128 devices in a mesh: dp: 4 (over x), fy: 4 (over z_hi, core), fx: 8 (over z_lo, y).
Axes of the slice: x: 4, y: 4, z: 4 (z_hi: 2, z_lo: 2; z = z_hi * 2 + z_lo), core: 2. Of those that a mesh axis runs over, the one named last changes fastest.
Arguments:
- fine_tokens: bfloat16 [4, 64, 256, 768], P('dp', 'fy', 'fx'), may hold values from -40 to 40
- parent: int32 [4, 64, 64], P('dp', 'fy', 'fx'), may hold values from 0 to 511, as said below
- coarse_tokens: bfloat16 [4, 512, 768], P('dp', 'fx'), may hold values from -6 to 6
- tile_level: int32 [4, 512], P('dp', 'fx'), may hold values from 0 to 2
- level_table: float32 [3, 768], replicated, may hold values from -3 to 3
- norm_gain: float32 [768], replicated, may hold values from 0.5 to 1.5
- qkv_weight: bfloat16 [768, 2304], replicated, may hold values from -7 to 7
- out_weight: bfloat16 [768, 768], replicated, may hold values from -0.21875 to 0.21875
- cotangent: bfloat16 [4, 64, 256, 768], P('dp', 'fy', 'fx'), may hold values from -6 to 6
Outputs:
- mixed: bfloat16 [4, 64, 256, 768], P('dp', 'fy', 'fx')
- grad_tokens: bfloat16 [4, 64, 256, 768], P('dp', 'fy', 'fx')
- grad_coarse: float32 [4, 512, 768], P('dp', 'fx')
- grad_qkv: float32 [768, 2304], P('dp')
- grad_out: float32 [768, 768], P('dp')
- grad_gain: float32 [768], P('dp')
- grad_level: float32 [3, 768], replicated
The draws below stay inside these ranges and needn't reach their ends.
Inputs may be any that keep to these rules, and one draw needn't show every extreme that they name: `parent`: each entry names a coarse token of the same frame; a token of level l is drawn with weight l + 1.
All inputs are finite; a program needn't handle non-finite values.
Results may differ from the reference program's by a relative error of at most 0.025.
Values may be sent and summed in bfloat16 or wider, within the bound.
A program may use at most 128 MiB of HBM per device.

```python
import math
import jax
import jax.numpy as jnp
from jax import lax

D = 768
HEADS = 12
BLK = 4
LEVELS = 3
FRAMES = 4
NY = 64
NX = 256
NCOARSE = 512


def locate(bounds_row, picks_frame):
    return jnp.searchsorted(bounds_row, picks_frame, side='right').astype(jnp.int32)


def routing_tables(key):
    level_key = jax.random.fold_in(key, 11)
    pick_key = jax.random.fold_in(key, 12)
    levels = jax.random.randint(level_key, (FRAMES, NCOARSE), 0, LEVELS).astype(jnp.int32)
    bounds = jnp.cumsum(levels + 1, axis=1).astype(jnp.int32)
    totals = bounds[:, -1]
    picks = jax.random.randint(pick_key, (FRAMES, NY, NX // BLK), 0, totals[:, None, None]).astype(jnp.int32)
    parents = jax.vmap(locate)(bounds, picks)
    return (levels, parents)


def draw_parent(key, part):
    return routing_tables(key)[1]


def draw_tile_level(key, part):
    return routing_tables(key)[0]


def draw_fine_tokens(key, part):
    noise_key = jax.random.fold_in(key, 21)
    row_key = jax.random.fold_in(key, 22)
    column_key = jax.random.fold_in(key, 23)
    noise = jnp.clip(jax.random.normal(noise_key, (FRAMES, NY, NX, D), jnp.float32), -4.0, 4.0)
    row_scale = 0.3 * jnp.exp(jax.random.uniform(row_key, (FRAMES, NY, NX, 1), jnp.float32) * math.log(10.0))
    column_scale = 0.3 * jnp.exp(jax.random.uniform(column_key, (D,), jnp.float32) * math.log(10.0))
    values = noise * row_scale * column_scale
    return values.astype(jnp.bfloat16)


def draw_qkv_weight(key, part):
    base_key = jax.random.fold_in(key, 31)
    base = jnp.clip(jax.random.normal(base_key, (D, 3 * D), jnp.float32), -4.0, 4.0) * D ** (-0.5)
    return base.astype(jnp.bfloat16)


def block_levels(rng, dims, shards, low, high):
    def one(dim, parts):
        draws = jax.random.uniform(jax.random.fold_in(jax.random.fold_in(rng, 6), dim), (parts,), jnp.float32, low / len(shards), high / len(shards))
        return jnp.repeat(jnp.exp(draws), dims[dim] // parts).reshape((-1,) + (1,) * (len(dims) - dim - 1))

    gain = one(*shards[0])
    for cut in shards[1:]:
        gain = gain * one(*cut)
    return gain


def scatter_about(key, shape, spread, reach, cuts=(), dtype=jnp.bfloat16):
    loudness = block_levels(key, shape, cuts, -0.22, 0.18) if cuts else 1.0
    result = jax.random.normal(key, shape, jnp.float32) * spread * loudness
    return jnp.minimum(jnp.maximum(result, -reach), reach).astype(dtype)


def setup_inputs(seed: int = 0) -> dict:
    seeds = jax.random.split(jax.random.key(seed), 10)
    fine_tokens = draw_fine_tokens(jax.random.fold_in(seeds[9], 71), 0)
    parent = draw_parent(jax.random.fold_in(seeds[9], 71), 0)
    coarse_tokens = scatter_about(seeds[2], (FRAMES, NCOARSE, D), 1.0, 6.0, ((0, 4), (1, 8)))
    tile_level = draw_tile_level(jax.random.fold_in(seeds[9], 71), 0)
    level_table = scatter_about(seeds[4], (LEVELS, D), 0.5, 3.0, (), jnp.float32)
    norm_gain = jnp.clip(1.0 + 0.1 * jax.random.normal(seeds[5], (D,), jnp.float32), 0.5, 1.5)
    qkv_weight = draw_qkv_weight(jax.random.fold_in(seeds[9], 71), 0)
    out_weight = scatter_about(seeds[7], (D, D), D ** -0.5, 0.21875)
    cotangent = scatter_about(seeds[8], (FRAMES, NY, NX, D), 1.0, 6.0, ((0, 4), (1, 4), (2, 8)))
    return {"fine_tokens": fine_tokens, "parent": parent, "coarse_tokens": coarse_tokens, "tile_level": tile_level, "level_table": level_table, "norm_gain": norm_gain, "qkv_weight": qkv_weight, "out_weight": out_weight, "cotangent": cotangent}


def attend_forward(queries, key_rows, values, score_scale, query_form, key_form, score_form):
    scores = jnp.einsum(query_form + ',' + key_form + '->' + score_form, queries.astype(jnp.float32), key_rows.astype(jnp.float32)) * score_scale
    weights = jax.nn.softmax(scores, axis=-1)
    rounded = weights.astype(jnp.bfloat16)
    attended = jnp.einsum(score_form + ',' + key_form + '->' + query_form, rounded.astype(jnp.float32), values.astype(jnp.float32))
    return attended.astype(jnp.bfloat16)

def attend_backward(queries, key_rows, values, grad_out, score_scale, query_form, key_form, score_form):
    scores = jnp.einsum(query_form + ',' + key_form + '->' + score_form, queries.astype(jnp.float32), key_rows.astype(jnp.float32)) * score_scale
    weights = jax.nn.softmax(scores, axis=-1)
    rounded = weights.astype(jnp.bfloat16)
    grad_values = jnp.einsum(score_form + ',' + query_form + '->' + key_form, rounded.astype(jnp.float32), grad_out.astype(jnp.float32)).astype(jnp.bfloat16)
    grad_weights = jnp.einsum(query_form + ',' + key_form + '->' + score_form, grad_out.astype(jnp.float32), values.astype(jnp.float32))
    inner = lax.optimization_barrier(jnp.sum(weights * grad_weights, axis=-1, keepdims=True))
    grad_scores = (weights * (grad_weights - inner) * score_scale).astype(jnp.bfloat16)
    grad_queries = jnp.einsum(score_form + ',' + key_form + '->' + query_form, grad_scores.astype(jnp.float32), key_rows.astype(jnp.float32)).astype(jnp.bfloat16)
    grad_keys = jnp.einsum(score_form + ',' + query_form + '->' + key_form, grad_scores.astype(jnp.float32), queries.astype(jnp.float32)).astype(jnp.bfloat16)
    return (grad_queries, grad_keys, grad_values)

def split_heads(tensor, head_dim):
    return tensor.reshape(tensor.shape[0], tensor.shape[1], -1, head_dim)

def one_frame(fine_rows, parent_ids, coarse_rows, levels, cotangent_rows, level_table, norm_gain, qkv_weight, out_weight):
    half_width = D // 2
    head_dim = D // HEADS
    score_scale = head_dim ** (-0.5)
    summary = (coarse_rows.astype(jnp.float32) + level_table[levels]).astype(jnp.bfloat16)
    read_rows = summary[parent_ids].astype(jnp.float32)
    residual = fine_rows.astype(jnp.float32) + jnp.repeat(read_rows, BLK, axis=1)
    inv_rms = lax.rsqrt(lax.optimization_barrier(jnp.mean(residual * residual, axis=-1, keepdims=True)) + 1e-06)
    normed_pre = residual * inv_rms
    normed = (normed_pre * norm_gain).astype(jnp.bfloat16)
    flat_normed = normed.reshape(NY * NX, D)
    projected = jnp.dot(flat_normed, qkv_weight, preferred_element_type=jnp.float32).astype(jnp.bfloat16).reshape(NY, NX, 3 * D)
    row_query = split_heads(projected[..., 0:half_width], head_dim)
    column_query = split_heads(projected[..., half_width:D], head_dim)
    row_key = split_heads(projected[..., D:D + half_width], head_dim)
    column_key = split_heads(projected[..., D + half_width:2 * D], head_dim)
    row_value = split_heads(projected[..., 2 * D:2 * D + half_width], head_dim)
    column_value = split_heads(projected[..., 2 * D + half_width:3 * D], head_dim)
    row_out = attend_forward(row_query, row_key, row_value, score_scale, 'bqhd', 'bkhd', 'bhqk')
    column_out = attend_forward(column_query, column_key, column_value, score_scale, 'qbhd', 'kbhd', 'bhqk')
    attended = jnp.concatenate([row_out.reshape(NY, NX, half_width), column_out.reshape(NY, NX, half_width)], axis=-1)
    flat_att = attended.reshape(NY * NX, D)
    out_proj = jnp.dot(flat_att, out_weight, preferred_element_type=jnp.float32)
    mixed = (residual + out_proj.reshape(NY, NX, D)).astype(jnp.bfloat16)
    flat_cot = cotangent_rows.reshape(NY * NX, D)
    grad_att = jnp.dot(flat_cot, out_weight.T, preferred_element_type=jnp.float32).astype(jnp.bfloat16).reshape(NY, NX, D)
    grad_out_weight = jnp.dot(flat_att.T, flat_cot, preferred_element_type=jnp.float32)
    row_grads = attend_backward(row_query, row_key, row_value, split_heads(grad_att[..., 0:half_width], head_dim), score_scale, 'bqhd', 'bkhd', 'bhqk')
    column_grads = attend_backward(column_query, column_key, column_value, split_heads(grad_att[..., half_width:D], head_dim), score_scale, 'qbhd', 'kbhd', 'bhqk')
    pieces = []
    for which in range(3):
        pieces.append(row_grads[which].reshape(NY, NX, half_width))
        pieces.append(column_grads[which].reshape(NY, NX, half_width))
    grad_projected = jnp.concatenate(pieces, axis=-1).reshape(NY * NX, 3 * D)
    grad_normed = jnp.dot(grad_projected, qkv_weight.T, preferred_element_type=jnp.float32)
    grad_qkv_weight = jnp.dot(flat_normed.T, grad_projected, preferred_element_type=jnp.float32)
    flat_pre = normed_pre.reshape(NY * NX, D)
    grad_gain = lax.optimization_barrier(jnp.sum(grad_normed * flat_pre, axis=0))
    grad_pre = grad_normed * norm_gain
    flat_inv = inv_rms.reshape(NY * NX, 1)
    grad_residual = flat_inv * (grad_pre - flat_pre * lax.optimization_barrier(jnp.mean(grad_pre * flat_pre, axis=-1, keepdims=True))) + flat_cot.astype(jnp.float32)
    grad_fine = grad_residual.astype(jnp.bfloat16).reshape(NY, NX, D)
    block_grad = grad_residual.reshape(NY, NX // BLK, BLK, D).sum(axis=2).reshape(-1, D)
    grad_coarse = jax.ops.segment_sum(block_grad, parent_ids.reshape(-1), num_segments=NCOARSE)
    grad_level = jax.ops.segment_sum(grad_coarse, levels, num_segments=LEVELS)
    return (mixed, grad_fine, grad_coarse, grad_qkv_weight, grad_out_weight, grad_gain, grad_level)

def reference(fine_tokens, parent, coarse_tokens, tile_level, level_table, norm_gain, qkv_weight, out_weight, cotangent):

    def frame_step(totals, frame_data):
        fine_rows, parent_ids, coarse_rows, levels, cotangent_rows = frame_data
        results = one_frame(fine_rows, parent_ids, coarse_rows, levels, cotangent_rows, level_table, norm_gain, qkv_weight, out_weight)
        totals = (totals[0] + results[3], totals[1] + results[4], totals[2] + results[5], totals[3] + results[6])
        return (totals, (results[0], results[1], results[2]))
    initial = (jnp.zeros((D, 3 * D), jnp.float32), jnp.zeros((D, D), jnp.float32), jnp.zeros((D,), jnp.float32), jnp.zeros((LEVELS, D), jnp.float32))
    totals, stacked = lax.scan(frame_step, initial, (fine_tokens, parent, coarse_tokens, tile_level, cotangent))
    grad_scale = 1.0 / math.sqrt(FRAMES * NY * NX)
    return (stacked[0], stacked[1], stacked[2], totals[0] * grad_scale, totals[1] * grad_scale, totals[2] * grad_scale, totals[3] * grad_scale)
```

```python
import functools
import math

import jax
import jax.numpy as jnp
from jax import lax
from jax.experimental import pallas as pl
from jax.experimental.pallas import tpu as pltpu
from jax.sharding import PartitionSpec as P

HEADS = 12
BLK = 4
LEVELS = 3
MESH = pl.DeviceIdType.MESH
F32 = jnp.float32
BF16 = jnp.bfloat16
FXP = [(a, b) for a in range(2) for b in range(4) if (a, b) != (0, 0)]
FYP = [(0, 1), (1, 0), (1, 1)]
YZP = [(a, b) for a in range(4) for b in range(4) if (a, b) != (0, 0)]
LANES = 128


def dims(a, b, ca, cb):
    return lax.dot_general(a, b, (((ca,), (cb,)), ((), ())), preferred_element_type=F32)


class Place:
    def __init__(self):
        self.dp = lax.axis_index("dp")
        self.fy = lax.axis_index("fy")
        self.fx = lax.axis_index("fx")
        self.zh, self.core = self.fy // 2, self.fy % 2
        self.zl, self.y = self.fx // 4, self.fx % 4
        self.z = self.zh * 2 + self.zl

    def fx_at(self, a, b):
        return lax.rem(self.zl + a, 2) * 4 + lax.rem(self.y + b, 4)

    def fy_at(self, a, c):
        return lax.rem(self.zh + a, 2) * 2 + lax.rem(self.core + c, 2)

    def yz(self, a, b):
        z, y = lax.rem(self.z + a, 4), lax.rem(self.y + b, 4)
        dev = {"fy": (z // 2) * 2 + self.core, "fx": (z % 2) * 4 + y}
        return dev, z * 4 + y

    def dp_at(self, d):
        return lax.rem(self.dp + d, 4)


def rcopy(src, dst, ss, rs, dev):
    return pltpu.make_async_remote_copy(
        src_ref=src, dst_ref=dst, send_sem=ss, recv_sem=rs, device_id=dev, device_id_type=MESH
    )


def greet(devs):
    barrier = pltpu.get_barrier_semaphore()
    for dev in devs:
        pl.semaphore_signal(barrier, inc=1, device_id=dev, device_id_type=MESH)
    pl.semaphore_wait(barrier, len(devs))


def onehot(cond):
    return jnp.where(cond, 1.0, 0.0).astype(BF16)


def to_columns(rows, cols):
    n = rows * cols
    new = lax.broadcasted_iota(jnp.int32, (n, n), 0)
    old = lax.broadcasted_iota(jnp.int32, (n, n), 1)
    return onehot(old == lax.rem(new, rows) * cols + new // rows)


def front_kernel(
    rows, cols, fine, cot, ptok, coarse, level, table, gain, wo,
    rown, rowd, coln, cold, res, lv,
    tab, sn, sd, snc, sdc,
    ag_s, ag_r, fw_s, fw_r, row_s, row_r, col_s, col_r, loc,
):
    at = Place()
    n, width = fine.shape
    half = width // 2
    own = coarse.shape[0]
    part = own // 2
    mine = pl.ds(at.fx * own, own)
    lev = level[...]
    add = jnp.where(
        lev == 0, table[0:1, :], jnp.where(lev == 1, table[1:2, :], table[2:3, :])
    )
    tab[mine, 0:width] = (coarse[...].astype(F32) + add).astype(BF16)
    lane = lax.broadcasted_iota(jnp.int32, (own, LANES), 1)
    tab[mine, width : width + LANES] = onehot(lane == lev + 1)
    fx_dev = [{"fx": at.fx_at(a, b)} for a, b in FXP]
    fy_dev = [{"fy": at.fy_at(a, c)} for a, c in FYP]
    greet(fx_dev + fy_dev)

    def chunk(owner, core):
        return tab.at[pl.ds(owner * own + core * part, part)]

    sent = []

    def go(c):
        c.start()
        sent.append(c)

    for i, dev in enumerate(fx_dev):
        go(rcopy(chunk(at.fx, at.core), chunk(at.fx, at.core), ag_s.at[i], ag_r.at[i], dev))

    def scatter(kind, src_row, dst_row, src_col, dst_col):
        rr, cc = src_row.shape[0] // 8, src_col.shape[0] // 4
        for i, (a, b) in enumerate(FXP):
            go(rcopy(
                src_row.at[pl.ds(at.fx_at(a, b) * rr, rr)], dst_row.at[:, pl.ds(at.fx * cols, cols)],
                row_s.at[kind, i], row_r.at[kind, i], fx_dev[i],
            ))
        for i, (a, c) in enumerate(FYP):
            go(rcopy(
                src_col.at[pl.ds(at.fy_at(a, c) * cc, cc)], dst_col.at[:, pl.ds(at.fy * rows, rows)],
                col_s.at[kind, i], col_r.at[kind, i], fy_dev[i],
            ))
        keep_row = pltpu.make_async_copy(
            src_row.at[pl.ds(at.fx * rr, rr)], dst_row.at[:, pl.ds(at.fx * cols, cols)], loc.at[kind, 0]
        )
        keep_col = pltpu.make_async_copy(
            src_col.at[pl.ds(at.fy * cc, cc)], dst_col.at[:, pl.ds(at.fy * rows, rows)], loc.at[kind, 1]
        )
        keep_row.start()
        keep_col.start()
        return [keep_row, keep_col]

    perm = to_columns(rows, cols)
    d = dims(cot[...], wo[...], 1, 1).astype(BF16)
    sd[...] = d[:, 0:half].reshape(rows, cols, half)
    sdc[...] = dims(perm, d[:, half:width], 1, 0).astype(BF16).reshape(cols, rows, half)
    kept = scatter(1, sd, rowd, sdc, cold)
    partner = {"fy": at.fy_at(0, 1)}
    for i, (a, b) in enumerate(FXP):
        src = at.fx_at(a, 4 - b)
        rcopy(chunk(src, at.core), chunk(src, at.core), ag_s.at[i], ag_r.at[i], fx_dev[i]).wait_recv()
        go(rcopy(chunk(src, at.core), chunk(src, at.core), fw_s.at[i], fw_r.at[i], partner))
    for i, (a, b) in enumerate(FXP):
        src = at.fx_at(a, 4 - b)
        rcopy(chunk(src, 1 - at.core), chunk(src, 1 - at.core), fw_s.at[i], fw_r.at[i], partner).wait_recv()
    pick = onehot(lax.broadcasted_iota(jnp.int32, (n, tab.shape[0]), 1) == ptok[...])
    read = dims(pick, tab[...], 1, 0)
    lv[...] = read[:, width : width + LANES].astype(BF16)
    residual = fine[...].astype(F32) + read[:, 0:width]
    res[...] = residual
    inv = lax.rsqrt(jnp.mean(residual * residual, axis=-1, keepdims=True) + 1e-06)
    normed = (residual * inv * gain[...]).astype(BF16)
    sn[...] = normed.reshape(rows, cols, width)
    snc[...] = dims(perm, normed, 1, 0).astype(BF16).reshape(cols, rows, width)
    kept += scatter(0, sn, rown, snc, coln)
    for kind, (dst_row, dst_col) in enumerate(((rown, coln), (rowd, cold))):
        for i, (a, b) in enumerate(FXP):
            ref = dst_row.at[:, pl.ds(at.fx_at(a, 4 - b) * cols, cols)]
            rcopy(ref, ref, row_s.at[kind, i], row_r.at[kind, i], fx_dev[i]).wait_recv()
        for i, (a, c) in enumerate(FYP):
            ref = dst_col.at[:, pl.ds(at.fy_at(a, c) * rows, rows)]
            rcopy(ref, ref, col_s.at[kind, i], col_r.at[kind, i], fy_dev[i]).wait_recv()
    for c in sent:
        c.wait_send()
    for c in kept:
        c.wait()


def front(fine, cot, ptok, coarse, level, table, gain, wo, rows, cols):
    n, width = fine.shape
    half = width // 2
    dma = pltpu.SemaphoreType.DMA
    wide = coarse.shape[0] * 8
    return pl.pallas_call(
        functools.partial(front_kernel, rows, cols),
        name="front",
        out_shape=[
            jax.ShapeDtypeStruct((rows // 8, cols * 8, width), BF16),
            jax.ShapeDtypeStruct((rows // 8, cols * 8, half), BF16),
            jax.ShapeDtypeStruct((cols // 4, rows * 4, width), BF16),
            jax.ShapeDtypeStruct((cols // 4, rows * 4, half), BF16),
            jax.ShapeDtypeStruct((n, width), F32),
            jax.ShapeDtypeStruct((n, LANES), BF16),
        ],
        in_specs=[pl.BlockSpec(memory_space=pltpu.VMEM)] * 8,
        out_specs=[pl.BlockSpec(memory_space=pltpu.VMEM)] * 6,
        scratch_shapes=[
            pltpu.VMEM((wide, width + LANES), BF16),
            pltpu.VMEM((rows, cols, width), BF16),
            pltpu.VMEM((rows, cols, half), BF16),
            pltpu.VMEM((cols, rows, width), BF16),
            pltpu.VMEM((cols, rows, half), BF16),
            dma((7,)), dma((7,)), dma((7,)), dma((7,)),
            dma((2, 7)), dma((2, 7)), dma((2, 3)), dma((2, 3)), dma((2, 2)),
        ],
        compiler_params=pltpu.CompilerParams(
            collective_id=0, has_side_effects=True, vmem_limit_bytes=48 << 20
        ),
    )(fine, cot, ptok, coarse, level, table, gain, wo)


def attend(q, k, v, d, scale, mask):
    size, lanes = q.shape
    first = lax.broadcasted_iota(jnp.int32, (size, lanes), 1) < lanes // 2

    def stack(t):
        zero = jnp.zeros_like(t)
        return jnp.concatenate([jnp.where(first, t, zero), jnp.where(first, zero, t)], axis=0)

    def join(t):
        return jnp.where(first, t[:size], t[size:])

    qs = stack((q.astype(F32) * scale).astype(BF16))
    ds_ = stack(d)
    s = dims(qs, k, 1, 1)
    if mask is not None:
        s = jnp.where(mask, s, -1e30)
    e = jnp.exp(s - jnp.max(s, axis=-1, keepdims=True))
    w = e * (1.0 / jnp.sum(e, axis=-1, keepdims=True))
    wb = w.astype(BF16)
    out = join(dims(wb, v, 1, 0)).astype(BF16)
    dv = dims(wb, ds_, 0, 0).astype(BF16)
    gw = dims(ds_, v, 1, 1)
    inner = jnp.sum(w * gw, axis=-1, keepdims=True)
    gs = (w * (gw - inner)).astype(BF16)
    dq = (join(dims(gs, k, 1, 0)) * scale).astype(BF16)
    dk = dims(gs, qs, 0, 0).astype(BF16)
    return out, dq, dk, dv


def attention_kernel(
    scale, col_rows, rown, rowd, coln, cold, wq, orow, gnr, ocol, gnc, w2, qkv, grads
):
    half = rowd.shape[1]
    for which, (x, d, out, gn) in enumerate(((rown, rowd, orow, gnr), (coln, cold, ocol, gnc))):
        for j in range(3):
            c0 = (2 * j + which) * half
            qkv[:, j * half : (j + 1) * half] = dims(x[...], wq[:, c0 : c0 + half], 1, 0).astype(BF16)
        size = 256 if which == 0 else 2 * col_rows
        mask = None
        if which:
            i = lax.broadcasted_iota(jnp.int32, (2 * size, size), 0)
            j = lax.broadcasted_iota(jnp.int32, (2 * size, size), 1)
            mask = lax.rem(i, size) // col_rows == j // col_rows

        def one(u, _, d=d, out=out, size=size, mask=mask):
            t = pl.ds(pl.multiple_of(u * size, size), size)
            for p in range(half // LANES):
                c = p * LANES
                q, k, v = (qkv[t, j * half + c : j * half + c + LANES] for j in range(3))
                o, dq, dk, dv = attend(q, k, v, d[t, c : c + LANES], scale, mask)
                out[t, c : c + LANES] = o
                for j, g in enumerate((dq, dk, dv)):
                    grads[t, j * half + c : j * half + c + LANES] = g
            return 0

        lax.fori_loop(0, x.shape[0] // size, one, 0)
        total = None
        for j in range(3):
            c0 = (2 * j + which) * half
            g = grads[:, j * half : (j + 1) * half]
            back = dims(g, wq[:, c0 : c0 + half], 1, 1)
            total = back if total is None else total + back
            w2[which, :, j * half : (j + 1) * half] = dims(x[...], g, 0, 0).astype(BF16)
        gn[...] = total.astype(BF16)


def attention(rown, rowd, coln, cold, wq, scale, col_rows):
    n, width = rown.shape
    half = width // 2
    return pl.pallas_call(
        functools.partial(attention_kernel, scale, col_rows),
        name="attention",
        out_shape=[
            jax.ShapeDtypeStruct((n, half), BF16),
            jax.ShapeDtypeStruct((n, width), BF16),
            jax.ShapeDtypeStruct((n, half), BF16),
            jax.ShapeDtypeStruct((n, width), BF16),
            jax.ShapeDtypeStruct((2, width, 3 * half), BF16),
        ],
        in_specs=[pl.BlockSpec(memory_space=pltpu.VMEM)] * 5,
        out_specs=[pl.BlockSpec(memory_space=pltpu.VMEM)] * 5,
        scratch_shapes=[pltpu.VMEM((n, 3 * half), BF16), pltpu.VMEM((n, 3 * half), BF16)],
        compiler_params=pltpu.CompilerParams(vmem_limit_bytes=48 << 20),
    )(rown, rowd, coln, cold, wq)


class Reduce:
    @staticmethod
    def scratch(rows, nb):
        dma = pltpu.SemaphoreType.DMA
        piece = -(-(rows * nb // 16) // 16) * 16
        return [
            pltpu.VMEM((4 * rows, nb * LANES), BF16),
            pltpu.VMEM((3, rows, nb * LANES), BF16),
            pltpu.VMEM((3, rows, nb * LANES), BF16),
            pltpu.VMEM((rows, nb * LANES), F32),
            pltpu.VMEM((16 * piece, LANES), BF16),
            pltpu.VMEM((15, piece, LANES), BF16),
            pltpu.VMEM((2, 16 * piece, LANES), BF16),
            dma((2,)), dma((2,)), dma((3,)), dma((3,)), dma((15,)), dma((15,)), dma((15,)), dma((15,)),
        ]

    def __init__(self, at, refs, rows, nb):
        (self.cx, self.xs, self.xr, self.acc, self.p16, self.r16, self.ag,
         self.c_s, self.c_r, self.x_s, self.x_r, self.r_s, self.r_r, self.g_s, self.g_r) = refs
        self.at, self.rows, self.nb = at, rows, nb
        self.piece = self.r16.shape[1]
        self.partner = {"fy": at.fy_at(0, 1)}
        self.sent = []

    def go(self, c):
        c.start()
        self.sent.append(c)
        return c

    def swap(self, src):
        self.first = self.go(rcopy(src, self.cx, self.c_s.at[0], self.c_r.at[0], self.partner))

    def along_x(self, mine):
        self.first.wait_recv()
        for d in (2, 1, 3, 0):
            i = self.at.dp_at(d)
            block = pl.ds(pl.multiple_of(i * self.rows, self.rows), self.rows)
            value = mine(block) + self.cx[block, :].astype(F32)
            if d == 0:
                self.acc[...] = value
            else:
                self.xs[d - 1] = value.astype(BF16)
                self.go(rcopy(
                    self.xs.at[d - 1], self.xr.at[d - 1], self.x_s.at[d - 1], self.x_r.at[d - 1], {"dp": i}
                ))

    def scatter_yz(self):
        for d in range(3):
            rcopy(self.xs.at[d], self.xr.at[d], self.x_s.at[d], self.x_r.at[d], {"dp": self.at.dp}).wait_recv()
        rows = self.rows
        for b in range(self.nb):
            lanes = slice(b * LANES, (b + 1) * LANES)
            value = self.acc[:, lanes]
            for d in range(3):
                value = value + self.xr[d, :, lanes].astype(F32)
            self.p16[b * rows : (b + 1) * rows, :] = value.astype(BF16)
        used = self.nb * rows
        if used < self.p16.shape[0]:
            self.p16[used:, :] = jnp.zeros((self.p16.shape[0] - used, LANES), BF16)
        for i, (a, b) in enumerate(YZP):
            dev, q = self.at.yz(a, b)
            self.go(rcopy(self.p16.at[self.slot(q)], self.r16.at[i], self.r_s.at[i], self.r_r.at[i], dev))

    def slot(self, q):
        return pl.ds(pl.multiple_of(q * self.piece, self.piece), self.piece)

    def gather_yz(self):
        at = self.at
        _, q = at.yz(0, 0)
        value = self.p16[self.slot(q), :].astype(F32)
        for i in range(15):
            dev, _ = at.yz(*YZP[i])
            rcopy(self.r16.at[i], self.r16.at[i], self.r_s.at[i], self.r_r.at[i], dev).wait_recv()
            value = value + self.r16[i].astype(F32)
        self.ag[at.core, self.slot(q), :] = value.astype(BF16)
        src = self.ag.at[at.core, self.slot(q)]
        for i, (a, b) in enumerate(YZP):
            dev, _ = at.yz(a, b)
            self.go(rcopy(src, src, self.g_s.at[i], self.g_r.at[i], dev))

    def swap_back(self):
        at = self.at
        for i, (a, b) in enumerate(YZP):
            dev, q = at.yz(4 - a, 4 - b)
            ref = self.ag.at[at.core, self.slot(q)]
            rcopy(ref, ref, self.g_s.at[i], self.g_r.at[i], dev).wait_recv()
        ref = self.ag.at[at.core]
        self.go(rcopy(ref, ref, self.c_s.at[1], self.c_r.at[1], self.partner))

    def finish(self):
        ref = self.ag.at[1 - self.at.core]
        rcopy(ref, ref, self.c_s.at[1], self.c_r.at[1], self.partner).wait_recv()

    def block(self, half, b):
        return self.ag[half, b * self.rows : (b + 1) * self.rows, :].astype(F32)


def back_kernel(
    rows, cols, grad_scale, orow, gnr, ocol, gnc, w2,
    orow_t, gnr_t, ocol_t, gnc_t, gq,
    row_s, row_r, col_s, col_r, loc, *red,
):
    at = Place()
    width = gnr.shape[2]
    half = width // 2
    fx_dev = [{"fx": at.fx_at(a, b)} for a, b in FXP]
    fy_dev = [{"fy": at.fy_at(a, c)} for a, c in FYP]
    dp_dev = [{"dp": at.dp_at(d)} for d in (1, 2, 3)]
    greet(fx_dev + fy_dev + extra_devs(at) + dp_dev)
    sent = []
    weights = Reduce(at, red, width // 4, 3 * half // LANES)
    weights.swap(w2.at[1 - at.core])
    kinds = ((orow, orow_t, ocol, ocol_t), (gnr, gnr_t, gnc, gnc_t))
    kept = []
    for kind, (src_row, dst_row, src_col, dst_col) in enumerate(kinds):
        rr, cc = src_row.shape[0], src_col.shape[0]
        for i, (a, b) in enumerate(FXP):
            c = rcopy(
                src_row.at[:, pl.ds(at.fx_at(a, b) * cols, cols)], dst_row.at[pl.ds(at.fx * rr, rr)],
                row_s.at[kind, i], row_r.at[kind, i], fx_dev[i],
            )
            c.start()
            sent.append(c)
        for i, (a, b) in enumerate(FYP):
            c = rcopy(
                src_col.at[:, pl.ds(at.fy_at(a, b) * rows, rows)], dst_col.at[pl.ds(at.fy * cc, cc)],
                col_s.at[kind, i], col_r.at[kind, i], fy_dev[i],
            )
            c.start()
            sent.append(c)
        for i, (src, dst) in enumerate((
            (src_row.at[:, pl.ds(at.fx * cols, cols)], dst_row.at[pl.ds(at.fx * rr, rr)]),
            (src_col.at[:, pl.ds(at.fy * rows, rows)], dst_col.at[pl.ds(at.fy * cc, cc)]),
        )):
            c = pltpu.make_async_copy(src, dst, loc.at[kind, i])
            c.start()
            kept.append(c)
    weights.along_x(lambda block: w2[at.core, block, :].astype(F32))
    weights.scatter_yz()
    weights.gather_yz()
    weights.swap_back()
    weights.finish()
    for h in range(2):
        for j in range(3):
            for b in range(half // LANES):
                c0 = (2 * j + h) * half + b * LANES
                gq[:, c0 : c0 + LANES] = weights.block(h, j * (half // LANES) + b) * grad_scale
    for kind, (src_row, dst_row, src_col, dst_col) in enumerate(kinds):
        rr, cc = src_row.shape[0], src_col.shape[0]
        for i, (a, b) in enumerate(FXP):
            ref = dst_row.at[pl.ds(at.fx_at(a, 4 - b) * rr, rr)]
            rcopy(ref, ref, row_s.at[kind, i], row_r.at[kind, i], fx_dev[i]).wait_recv()
        for i, (a, b) in enumerate(FYP):
            ref = dst_col.at[pl.ds(at.fy_at(a, b) * cc, cc)]
            rcopy(ref, ref, col_s.at[kind, i], col_r.at[kind, i], fy_dev[i]).wait_recv()
    for c in sent + weights.sent:
        c.wait_send()
    for c in kept:
        c.wait()


def extra_devs(at):
    return [
        {"fy": at.fy_at(1, 0), "fx": at.fx_at(a, b)} for a, b in FXP
    ]


def back(orow, gnr, ocol, gnc, w2, rows, cols, grad_scale):
    width = gnr.shape[2]
    half = width // 2
    dma = pltpu.SemaphoreType.DMA
    return pl.pallas_call(
        functools.partial(back_kernel, rows, cols, grad_scale),
        name="back",
        out_shape=[
            jax.ShapeDtypeStruct((rows, cols, half), BF16),
            jax.ShapeDtypeStruct((rows, cols, width), BF16),
            jax.ShapeDtypeStruct((cols, rows, half), BF16),
            jax.ShapeDtypeStruct((cols, rows, width), BF16),
            jax.ShapeDtypeStruct((width // 4, 6 * half), F32),
        ],
        in_specs=[pl.BlockSpec(memory_space=pltpu.VMEM)] * 5,
        out_specs=[pl.BlockSpec(memory_space=pltpu.VMEM)] * 5,
        scratch_shapes=[
            dma((2, 7)), dma((2, 7)), dma((2, 3)), dma((2, 3)), dma((2, 2)),
            *Reduce.scratch(width // 4, 3 * half // LANES),
        ],
        compiler_params=pltpu.CompilerParams(
            collective_id=1, has_side_effects=True, vmem_limit_bytes=48 << 20
        ),
    )(orow, gnr, ocol, gnc, w2)


def post_kernel(
    rows, cols, grad_scale, orow, gnr, ocol, gnc, res, cot, ptok, lv, gain, wo,
    mixed, gfine, gcoarse, gout, small,
    att, go_out, go_own, co_out, co_in, co_own, cf_out, cf_in, cy_out, cy_in, gc16,
    sm_own, sm_in, sm_mid, sm_in2,
    co_s, co_r, cf_s, cf_r, cy_s, cy_r, s1_s, s1_r, s2_s, s2_r, *red,
):
    at = Place()
    n, width = gnr.shape
    half = width // 2
    own = gcoarse.shape[0]
    part = own // 2
    fx_dev = [{"fx": at.fx_at(a, b)} for a, b in FXP]
    fy_dev = [{"fy": at.fy_at(a, c)} for a, c in FYP]
    dp_off = [(d, c) for d in range(4) for c in range(2) if (d, c) != (0, 0)]
    dp_dev = [{"dp": at.dp_at(d), "fy": at.fy_at(0, c)} for d, c in dp_off]
    partner = fy_dev[0]
    greet(fx_dev + fy_dev[1:] + extra_devs(at) + dp_dev)
    sent = []

    def go(c):
        c.start()
        sent.append(c)
        return c

    perm = to_columns(rows, cols)
    att[:, 0:half] = orow[...]
    att[:, half:width] = dims(perm, ocol[...], 0, 0).astype(BF16)
    weights = Reduce(at, red, width // 4, half // LANES)

    def cot_half(h):
        return cot[:, pl.ds(pl.multiple_of(h * half, LANES), half)]

    go_out[...] = dims(att[...], cot_half(1 - at.core), 0, 0).astype(BF16)
    weights.swap(go_out)
    residual = res[...]
    grad_normed = gnr[...].astype(F32) + dims(perm, gnc[...], 0, 0)
    inv = lax.rsqrt(jnp.mean(residual * residual, axis=-1, keepdims=True) + 1e-06)
    pre = residual * inv
    sm_gain = jnp.sum(grad_normed * pre, axis=0, keepdims=True)
    g = grad_normed * gain[...]
    grad_residual = inv * (g - pre * jnp.mean(g * pre, axis=-1, keepdims=True)) + cot[...].astype(F32)
    gf = grad_residual.astype(BF16)
    gfine[...] = gf
    coarse_row = lax.broadcasted_iota(jnp.int32, (n, 8 * part), 1)

    def dense(core):
        named = coarse_row // part * own + lax.rem(coarse_row, part) + core * part
        return dims(onehot(named == ptok[...]), gf, 0, 0)

    co_out[...] = dense(1 - at.core).astype(BF16)
    go(rcopy(co_out, co_in, co_s.at[0], co_r.at[0], partner))
    go_own[...] = dims(att[...], cot_half(at.core), 0, 0)
    weights.along_x(lambda block: go_own[block, :])
    levels = dims(lv[...], gf, 0, 0)[0:8]
    row = lax.broadcasted_iota(jnp.int32, (8, half), 0)
    low = jnp.where(row == 0, sm_gain[:, 0:half], levels[:, 0:half])
    high = jnp.where(row == 0, sm_gain[:, half:width], levels[:, half:width])
    sm_own[0] = low
    sm_own[1] = high
    for i, dev in enumerate(dp_dev):
        go(rcopy(sm_own, sm_in.at[i], s1_s.at[i], s1_r.at[i], dev))
    co_own[...] = dense(at.core)
    rcopy(co_out, co_in, co_s.at[0], co_r.at[0], partner).wait_recv()
    for i, (a, b) in enumerate(FXP):
        owner = at.fx_at(a, b)
        block = pl.ds(pl.multiple_of(owner * part, part), part)
        cf_out[i] = (co_own[block, :] + co_in[block, :].astype(F32)).astype(BF16)
        go(rcopy(cf_out.at[i], cf_in.at[i], cf_s.at[i], cf_r.at[i], fx_dev[i]))
    mixed[...] = (residual + dims(att[...], wo[...], 1, 0)).astype(BF16)
    total = sm_own[...]
    for i, dev in enumerate(dp_dev):
        rcopy(sm_own, sm_in.at[i], s1_s.at[i], s1_r.at[i], dev).wait_recv()
        total = total + sm_in[i]
    sm_mid[...] = total
    for i, (a, b) in enumerate(YZP):
        go(rcopy(sm_mid, sm_in2.at[i], s2_s.at[i], s2_r.at[i], at.yz(a, b)[0]))
    weights.scatter_yz()
    block = pl.ds(pl.multiple_of(at.fx * part, part), part)
    value = co_own[block, :] + co_in[block, :].astype(F32)
    for i in range(7):
        rcopy(cf_out.at[i], cf_in.at[i], cf_s.at[i], cf_r.at[i], fx_dev[i]).wait_recv()
        value = value + cf_in[i].astype(F32)
    cy_out[...] = value.astype(BF16)
    for i, (a, c) in enumerate(FYP):
        go(rcopy(cy_out, cy_in.at[i], cy_s.at[i], cy_r.at[i], fy_dev[i]))
    weights.gather_yz()
    for i in range(3):
        rcopy(cy_out, cy_in.at[i], cy_s.at[i], cy_r.at[i], fy_dev[i]).wait_recv()
    mine = cy_out[...].astype(F32) + cy_in[1].astype(F32)
    other = cy_in[0].astype(F32) + cy_in[2].astype(F32)
    gcoarse[pl.ds(pl.multiple_of(at.core * part, part), part), :] = mine
    gcoarse[pl.ds(pl.multiple_of((1 - at.core) * part, part), part), :] = other
    total = sm_mid[...]
    for i, (a, b) in enumerate(YZP):
        rcopy(sm_mid, sm_in2.at[i], s2_s.at[i], s2_r.at[i], at.yz(a, b)[0]).wait_recv()
        total = total + sm_in2[i]
    small[...] = total * grad_scale
    weights.swap_back()
    weights.finish()
    for h in range(2):
        for b in range(half // LANES):
            c0 = h * half + b * LANES
            gout[:, c0 : c0 + LANES] = weights.block(h, b) * grad_scale
    for c in sent + weights.sent:
        c.wait_send()


def post(orow, gnr, ocol, gnc, res, cot, ptok, lv, gain, wo, own, rows, cols, grad_scale):
    n, width = gnr.shape
    half = width // 2
    part = own // 2
    dma = pltpu.SemaphoreType.DMA
    return pl.pallas_call(
        functools.partial(post_kernel, rows, cols, grad_scale),
        name="post",
        out_shape=[
            jax.ShapeDtypeStruct((n, width), BF16),
            jax.ShapeDtypeStruct((n, width), BF16),
            jax.ShapeDtypeStruct((own, width), F32),
            jax.ShapeDtypeStruct((width // 4, width), F32),
            jax.ShapeDtypeStruct((2, 8, half), F32),
        ],
        in_specs=[pl.BlockSpec(memory_space=pltpu.VMEM)] * 10,
        out_specs=[pl.BlockSpec(memory_space=pltpu.VMEM)] * 5,
        scratch_shapes=[
            pltpu.VMEM((n, width), BF16),
            pltpu.VMEM((width, half), BF16),
            pltpu.VMEM((width, half), F32),
            pltpu.VMEM((8 * part, width), BF16),
            pltpu.VMEM((8 * part, width), BF16),
            pltpu.VMEM((8 * part, width), F32),
            pltpu.VMEM((7, part, width), BF16),
            pltpu.VMEM((7, part, width), BF16),
            pltpu.VMEM((part, width), BF16),
            pltpu.VMEM((3, part, width), BF16),
            pltpu.VMEM((part, width), BF16),
            pltpu.VMEM((2, 8, half), F32),
            pltpu.VMEM((7, 2, 8, half), F32),
            pltpu.VMEM((2, 8, half), F32),
            pltpu.VMEM((15, 2, 8, half), F32),
            dma((1,)), dma((1,)), dma((7,)), dma((7,)), dma((3,)), dma((3,)),
            dma((7,)), dma((7,)), dma((15,)), dma((15,)),
            *Reduce.scratch(width // 4, half // LANES),
        ],
        compiler_params=pltpu.CompilerParams(
            collective_id=2, has_side_effects=True, vmem_limit_bytes=48 << 20
        ),
    )(orow, gnr, ocol, gnc, res, cot, ptok, lv, gain, wo)


def local(
    fine_tokens,
    parent,
    coarse_tokens,
    tile_level,
    level_table,
    norm_gain,
    qkv_weight,
    out_weight,
    cotangent,
):
    _, rows, cols, width = fine_tokens.shape
    half = width // 2
    n = rows * cols
    own = coarse_tokens.shape[1]
    scale = (width // HEADS) ** (-0.5)
    total_tokens = n * lax.axis_size("dp") * lax.axis_size("fy") * lax.axis_size("fx")
    grad_scale = 1.0 / math.sqrt(total_tokens)
    fine = fine_tokens.reshape(n, width)
    cot = cotangent.reshape(n, width)
    ptok = jnp.broadcast_to(parent.reshape(n // BLK, 1), (n // BLK, BLK)).reshape(n, 1)
    gain = norm_gain.reshape(1, width)
    rown, rowd, coln, cold, res, lv = front(
        fine, cot, ptok, coarse_tokens.reshape(own, width), tile_level.reshape(own, 1),
        level_table, gain, out_weight, rows, cols,
    )
    orow, gnr, ocol, gnc, w2 = attention(
        rown.reshape(n, width), rowd.reshape(n, half), coln.reshape(n, width), cold.reshape(n, half),
        qkv_weight, scale, rows * 4,
    )
    orow, gnr, ocol, gnc, gq = back(
        orow.reshape(rows // 8, cols * 8, half), gnr.reshape(rows // 8, cols * 8, width),
        ocol.reshape(cols // 4, rows * 4, half), gnc.reshape(cols // 4, rows * 4, width),
        w2, rows, cols, grad_scale,
    )
    mixed, gfine, gcoarse, gout, small = post(
        orow.reshape(n, half), gnr.reshape(n, width), ocol.reshape(n, half), gnc.reshape(n, width),
        res, cot, ptok, lv, gain, out_weight, own, rows, cols, grad_scale,
    )
    vectors = jnp.concatenate([small[0], small[1]], axis=-1)
    share = width // 4
    ggain = lax.dynamic_slice_in_dim(vectors[0], lax.axis_index("dp") * share, share)
    return (
        mixed.reshape(fine_tokens.shape),
        gfine.reshape(fine_tokens.shape),
        gcoarse[None],
        gq,
        gout,
        ggain,
        vectors[1 : 1 + LEVELS],
    )


def solution(mesh):
    return jax.shard_map(
        local,
        mesh=mesh,
        in_specs=(
            P("dp", "fy", "fx", None),
            P("dp", "fy", "fx"),
            P("dp", "fx", None),
            P("dp", "fx"),
            P(),
            P(),
            P(),
            P(),
            P("dp", "fy", "fx", None),
        ),
        out_specs=(
            P("dp", "fy", "fx", None),
            P("dp", "fy", "fx", None),
            P("dp", "fx", None),
            P("dp", None),
            P("dp", None),
            P("dp"),
            P(),
        ),
        check_vma=False,
    )
```

```python
import functools
import math

import jax
import jax.numpy as jnp
from jax import lax
from jax.experimental import pallas as pl
from jax.experimental.pallas import tpu as pltpu
from jax.sharding import PartitionSpec as P

HEADS = 12
BLK = 4
LEVELS = 3
MESH = pl.DeviceIdType.MESH
F32 = jnp.float32
BF16 = jnp.bfloat16
FXP = [(a, b) for a in range(2) for b in range(4) if (a, b) != (0, 0)]
FYP = [(0, 1), (1, 0), (1, 1)]
YZP = [(a, b) for a in range(4) for b in range(4) if (a, b) != (0, 0)]
LANES = 128


def dims(a, b, ca, cb):
    return lax.dot_general(a, b, (((ca,), (cb,)), ((), ())), preferred_element_type=F32)


class Place:
    def __init__(self):
        self.dp = lax.axis_index("dp")
        self.fy = lax.axis_index("fy")
        self.fx = lax.axis_index("fx")
        self.zh, self.core = self.fy // 2, self.fy % 2
        self.zl, self.y = self.fx // 4, self.fx % 4
        self.z = self.zh * 2 + self.zl

    def fx_at(self, a, b):
        return lax.rem(self.zl + a, 2) * 4 + lax.rem(self.y + b, 4)

    def fy_at(self, a, c):
        return lax.rem(self.zh + a, 2) * 2 + lax.rem(self.core + c, 2)

    def yz(self, a, b):
        z, y = lax.rem(self.z + a, 4), lax.rem(self.y + b, 4)
        dev = {"fy": (z // 2) * 2 + self.core, "fx": (z % 2) * 4 + y}
        return dev, z * 4 + y

    def dp_at(self, d):
        return lax.rem(self.dp + d, 4)


def rcopy(src, dst, ss, rs, dev):
    return pltpu.make_async_remote_copy(
        src_ref=src, dst_ref=dst, send_sem=ss, recv_sem=rs, device_id=dev, device_id_type=MESH
    )


def greet(devs):
    barrier = pltpu.get_barrier_semaphore()
    for dev in devs:
        pl.semaphore_signal(barrier, inc=1, device_id=dev, device_id_type=MESH)
    pl.semaphore_wait(barrier, len(devs))


def onehot(cond):
    return jnp.where(cond, 1.0, 0.0).astype(BF16)


def to_columns(rows, cols):
    n = rows * cols
    new = lax.broadcasted_iota(jnp.int32, (n, n), 0)
    old = lax.broadcasted_iota(jnp.int32, (n, n), 1)
    return onehot(old == lax.rem(new, rows) * cols + new // rows)


def attend(q, k, v, d, scale, mask):
    size, lanes = q.shape
    first = lax.broadcasted_iota(jnp.int32, (size, lanes), 1) < lanes // 2

    def stack(t):
        zero = jnp.zeros_like(t)
        return jnp.concatenate([jnp.where(first, t, zero), jnp.where(first, zero, t)], axis=0)

    def join(t):
        return jnp.where(first, t[:size], t[size:])

    qs = stack((q.astype(F32) * scale).astype(BF16))
    ds_ = stack(d)
    s = dims(qs, k, 1, 1)
    if mask is not None:
        s = jnp.where(mask, s, -1e30)
    e = jnp.exp(s - jnp.max(s, axis=-1, keepdims=True))
    w = e * (1.0 / jnp.sum(e, axis=-1, keepdims=True))
    wb = w.astype(BF16)
    out = join(dims(wb, v, 1, 0)).astype(BF16)
    dv = dims(wb, ds_, 0, 0).astype(BF16)
    gw = dims(ds_, v, 1, 1)
    inner = jnp.sum(w * gw, axis=-1, keepdims=True)
    gs = (w * (gw - inner)).astype(BF16)
    dq = (join(dims(gs, k, 1, 0)) * scale).astype(BF16)
    dk = dims(gs, qs, 0, 0).astype(BF16)
    return out, dq, dk, dv


class Reduce:
    @staticmethod
    def scratch(rows, nb):
        dma = pltpu.SemaphoreType.DMA
        piece = -(-(rows * nb // 16) // 16) * 16
        return [
            pltpu.VMEM((4 * rows, nb * LANES), BF16),
            pltpu.VMEM((3, rows, nb * LANES), BF16),
            pltpu.VMEM((3, rows, nb * LANES), BF16),
            pltpu.VMEM((rows, nb * LANES), F32),
            pltpu.VMEM((16 * piece, LANES), BF16),
            pltpu.VMEM((15, piece, LANES), BF16),
            pltpu.VMEM((2, 16 * piece, LANES), BF16),
            dma((2,)), dma((2,)), dma((3,)), dma((3,)), dma((15,)), dma((15,)), dma((15,)), dma((15,)),
        ]

    def __init__(self, at, refs, rows, nb):
        (self.cx, self.xs, self.xr, self.acc, self.p16, self.r16, self.ag,
         self.c_s, self.c_r, self.x_s, self.x_r, self.r_s, self.r_r, self.g_s, self.g_r) = refs
        self.at, self.rows, self.nb = at, rows, nb
        self.piece = self.r16.shape[1]
        self.partner = {"fy": at.fy_at(0, 1)}

    def go(self, c):
        c.start()

    def swap(self, src):
        return rcopy(src, self.cx, self.c_s.at[0], self.c_r.at[0], self.partner)

    def drain(self):
        rcopy(self.cx, self.cx, self.c_s.at[0], self.c_r.at[0], self.partner).wait_send()
        ref = self.ag.at[self.at.core]
        rcopy(ref, ref, self.c_s.at[1], self.c_r.at[1], self.partner).wait_send()
        for d in range(3):
            rcopy(self.xs.at[d], self.xr.at[d], self.x_s.at[d], self.x_r.at[d], self.partner).wait_send()
        for i in range(15):
            ref = self.r16.at[i]
            rcopy(ref, ref, self.r_s.at[i], self.r_r.at[i], self.partner).wait_send()
            rcopy(ref, ref, self.g_s.at[i], self.g_r.at[i], self.partner).wait_send()

    def along_x(self, mine):
        self.swap(self.cx).wait_recv()
        for d in (2, 1, 3, 0):
            i = self.at.dp_at(d)
            block = pl.ds(pl.multiple_of(i * self.rows, self.rows), self.rows)
            value = mine(block) + self.cx[block, :].astype(F32)
            if d == 0:
                self.acc[...] = value
            else:
                self.xs[d - 1] = value.astype(BF16)
                self.go(rcopy(
                    self.xs.at[d - 1], self.xr.at[d - 1], self.x_s.at[d - 1], self.x_r.at[d - 1], {"dp": i}
                ))

    def scatter_yz(self):
        for d in range(3):
            rcopy(self.xs.at[d], self.xr.at[d], self.x_s.at[d], self.x_r.at[d], {"dp": self.at.dp}).wait_recv()
        rows = self.rows
        for b in range(self.nb):
            lanes = slice(b * LANES, (b + 1) * LANES)
            value = self.acc[:, lanes]
            for d in range(3):
                value = value + self.xr[d, :, lanes].astype(F32)
            self.p16[b * rows : (b + 1) * rows, :] = value.astype(BF16)
        used = self.nb * rows
        if used < self.p16.shape[0]:
            self.p16[used:, :] = jnp.zeros((self.p16.shape[0] - used, LANES), BF16)
        for i, (a, b) in enumerate(YZP):
            dev, q = self.at.yz(a, b)
            self.go(rcopy(self.p16.at[self.slot(q)], self.r16.at[i], self.r_s.at[i], self.r_r.at[i], dev))

    def slot(self, q):
        return pl.ds(pl.multiple_of(q * self.piece, self.piece), self.piece)

    def gather_yz(self):
        at = self.at
        _, q = at.yz(0, 0)
        value = self.p16[self.slot(q), :].astype(F32)
        for i in range(15):
            dev, _ = at.yz(*YZP[i])
            rcopy(self.r16.at[i], self.r16.at[i], self.r_s.at[i], self.r_r.at[i], dev).wait_recv()
            value = value + self.r16[i].astype(F32)
        self.ag[at.core, self.slot(q), :] = value.astype(BF16)
        src = self.ag.at[at.core, self.slot(q)]
        for i, (a, b) in enumerate(YZP):
            dev, _ = at.yz(a, b)
            self.go(rcopy(src, src, self.g_s.at[i], self.g_r.at[i], dev))

    def swap_back(self):
        at = self.at
        for i, (a, b) in enumerate(YZP):
            dev, q = at.yz(4 - a, 4 - b)
            ref = self.ag.at[at.core, self.slot(q)]
            rcopy(ref, ref, self.g_s.at[i], self.g_r.at[i], dev).wait_recv()
        ref = self.ag.at[at.core]
        self.go(rcopy(ref, ref, self.c_s.at[1], self.c_r.at[1], self.partner))

    def finish(self):
        ref = self.ag.at[1 - self.at.core]
        rcopy(ref, ref, self.c_s.at[1], self.c_r.at[1], self.partner).wait_recv()

    def block(self, half, b):
        return self.ag[half, b * self.rows : (b + 1) * self.rows, :].astype(F32)


class Legs:
    def __init__(self, at, rows, cols, sems):
        self.at, self.rows, self.cols = at, rows, cols
        self.row_s, self.row_r, self.col_s, self.col_r, self.loc = sems
        self.fx_dev = [{"fx": at.fx_at(a, b)} for a, b in FXP]
        self.fy_dev = [{"fy": at.fy_at(a, c)} for a, c in FYP]
        self.sent = []
        self.kept = []

    def send(self, src, dst, ss, rs, dev):
        c = rcopy(src, dst, ss, rs, dev)
        c.start()
        self.sent.append(c)

    def keep(self, src, dst, sem):
        c = pltpu.make_async_copy(src, dst, sem)
        c.start()
        return c

    def token_row(self, ref, u, owner):
        return ref.at[pl.ds(owner * 2 + u, 1)]

    def token_col(self, ref, u, owner):
        return ref.at[pl.ds(owner * (self.cols // 4) + u * (self.cols // 8), self.cols // 8)]

    def owner_row(self, ref, u, member):
        return ref.at[pl.ds(u, 1), pl.ds(member * self.cols, self.cols)]

    def owner_col(self, ref, u, member):
        return ref.at[pl.ds(u * (self.cols // 8), self.cols // 8), pl.ds(member * self.rows, self.rows)]

    def out_row(self, kind, u, src, dst):
        at = self.at
        for i, (a, b) in enumerate(FXP):
            self.send(
                self.token_row(src, u, at.fx_at(a, b)), self.owner_row(dst, u, at.fx),
                self.row_s.at[kind, u, i], self.row_r.at[kind, u, i], self.fx_dev[i],
            )
        return self.keep(self.token_row(src, u, at.fx), self.owner_row(dst, u, at.fx), self.loc.at[kind, u])

    def out_col(self, kind, u, src, dst):
        at = self.at
        for i, (a, c) in enumerate(FYP):
            self.send(
                self.token_col(src, u, at.fy_at(a, c)), self.owner_col(dst, u, at.fy),
                self.col_s.at[kind, u, i], self.col_r.at[kind, u, i], self.fy_dev[i],
            )
        return self.keep(self.token_col(src, u, at.fy), self.owner_col(dst, u, at.fy), self.loc.at[kind, 2 + u])

    def got_row(self, kind, u, dst):
        for i, (a, b) in enumerate(FXP):
            ref = self.owner_row(dst, u, self.at.fx_at(a, 4 - b))
            rcopy(ref, ref, self.row_s.at[kind, u, i], self.row_r.at[kind, u, i], self.fx_dev[i]).wait_recv()

    def got_col(self, kind, u, dst):
        for i, (a, c) in enumerate(FYP):
            ref = self.owner_col(dst, u, self.at.fy_at(a, c))
            rcopy(ref, ref, self.col_s.at[kind, u, i], self.col_r.at[kind, u, i], self.fy_dev[i]).wait_recv()

    def home_row(self, kind, u, src, dst):
        at = self.at
        for i, (a, b) in enumerate(FXP):
            self.send(
                self.owner_row(src, u, at.fx_at(a, b)), self.token_row(dst, u, at.fx),
                self.row_s.at[kind, u, i], self.row_r.at[kind, u, i], self.fx_dev[i],
            )
        return self.keep(self.owner_row(src, u, at.fx), self.token_row(dst, u, at.fx), self.loc.at[kind, u])

    def home_col(self, kind, u, src, dst):
        at = self.at
        for i, (a, c) in enumerate(FYP):
            self.send(
                self.owner_col(src, u, at.fy_at(a, c)), self.token_col(dst, u, at.fy),
                self.col_s.at[kind, u, i], self.col_r.at[kind, u, i], self.fy_dev[i],
            )
        return self.keep(self.owner_col(src, u, at.fy), self.token_col(dst, u, at.fy), self.loc.at[kind, 2 + u])

    def back_row(self, kind, u, dst):
        for i, (a, b) in enumerate(FXP):
            ref = self.token_row(dst, u, self.at.fx_at(a, 4 - b))
            rcopy(ref, ref, self.row_s.at[kind, u, i], self.row_r.at[kind, u, i], self.fx_dev[i]).wait_recv()

    def back_col(self, kind, u, dst):
        for i, (a, c) in enumerate(FYP):
            ref = self.token_col(dst, u, self.at.fy_at(a, c))
            rcopy(ref, ref, self.col_s.at[kind, u, i], self.col_r.at[kind, u, i], self.fy_dev[i]).wait_recv()


def extra_devs(at):
    return [{"fy": at.fy_at(1, 0), "fx": at.fx_at(a, b)} for a, b in FXP]


N_RED = 15


def layer_kernel(
    rows, cols, scale, grad_scale, fine_h, cot_h, ptok, coarse, level, table, gain, wq_h, wo_h,
    mixed, gfine, gcoarse, gq, gout, small,
    fine, cot, wq, wo, tab, perm, res, lv,
    sn, sd, snc, sdc, rown, rowd, coln, cold, qkv, grads, w2,
    orow, gnr, ocol, gnc, orow_t, gnr_t, ocol_t, gnc_t, dd, oo, gg,
    att, go_out, go_own, co_out, co_in, co_own, cf_out, cf_in, cy_out, cy_in,
    sm_own, sm_in, sm_mid, sm_in2,
    ld, ag_s, ag_r, fw_s, fw_r, row_s, row_r, col_s, col_r, loc,
    co_s, co_r, cf_s, cf_r, cy_s, cy_r, s1_s, s1_r, s2_s, s2_r, *red,
):
    at = Place()
    n, width = fine.shape
    half = width // 2
    own = coarse.shape[0]
    part = own // 2
    legs = Legs(at, rows, cols, (row_s, row_r, col_s, col_r, loc))
    fx_dev, fy_dev = legs.fx_dev, legs.fy_dev
    partner = fy_dev[0]
    dp_off = [(d, c) for d in range(4) for c in range(2) if (d, c) != (0, 0)]
    dp_dev = [{"dp": at.dp_at(d), "fy": at.fy_at(0, c)} for d, c in dp_off]
    weights = Reduce(at, red[:N_RED], width // 4, 3 * half // LANES)
    outs = Reduce(at, red[N_RED:], width // 4, half // LANES)
    sent = legs.sent
    go = legs.send

    loads = [
        pltpu.make_async_copy(a, b, ld.at[i])
        for i, (a, b) in enumerate(((cot_h, cot), (wo_h, wo), (fine_h, fine), (wq_h, wq)))
    ]
    for c in loads:
        c.start()
    mine = pl.ds(at.fx * own, own)
    lev = level[...]
    add = jnp.where(lev == 0, table[0:1, :], jnp.where(lev == 1, table[1:2, :], table[2:3, :]))
    tab[mine, 0:width] = (coarse[...].astype(F32) + add).astype(BF16)
    lane = lax.broadcasted_iota(jnp.int32, (own, LANES), 1)
    tab[mine, width : width + LANES] = onehot(lane == lev + 1)
    perm[...] = to_columns(rows, cols)
    greet(fx_dev + fy_dev[1:] + extra_devs(at) + dp_dev)

    def chunk(owner, core):
        return tab.at[pl.ds(owner * own + core * part, part)]

    def across(a, b):
        fx = at.fx_at(a, b)
        return {"fx": fx} if a == 0 else {"fx": fx, "fy": at.fy_at(at.core, 0)}

    for i, (a, b) in enumerate(FXP):
        go(chunk(at.fx, at.core), chunk(at.fx, at.core), ag_s.at[i], ag_r.at[i], across(a, b))
    loads[0].wait()
    loads[1].wait()
    d = dims(cot[...], wo[...], 1, 1).astype(BF16)
    sd[...] = d[:, 0:half].reshape(rows, cols, half)
    kept = [legs.out_row(1, u, sd, rowd) for u in range(2)]
    sdc[...] = dims(perm[...], d[:, half:width], 1, 0).astype(BF16).reshape(cols, rows, half)
    kept += [legs.out_col(1, u, sdc, cold) for u in range(2)]
    for i, (a, b) in enumerate(FXP):
        src = chunk(at.fx_at(a, 4 - b), at.core)
        rcopy(src, src, ag_s.at[i], ag_r.at[i], across(a, b)).wait_recv()
        go(src, src, fw_s.at[i], fw_r.at[i], partner)
    loads[2].wait()
    for i, (a, b) in enumerate(FXP):
        src = chunk(at.fx_at(a, 4 - b), 1 - at.core)
        rcopy(src, src, fw_s.at[i], fw_r.at[i], partner).wait_recv()
    pick = onehot(lax.broadcasted_iota(jnp.int32, (n, tab.shape[0]), 1) == ptok[...])
    read = dims(pick, tab[...], 1, 0)
    lv[...] = read[:, width : width + LANES].astype(BF16)
    residual = fine[...].astype(F32) + read[:, 0:width]
    res[...] = residual
    inv = lax.rsqrt(jnp.mean(residual * residual, axis=-1, keepdims=True) + 1e-06)
    normed = (residual * inv * gain[...]).astype(BF16)
    sn[...] = normed.reshape(rows, cols, width)
    kept += [legs.out_row(0, u, sn, rown) for u in range(2)]
    snc[...] = dims(perm[...], normed, 1, 0).astype(BF16).reshape(cols, rows, width)
    kept += [legs.out_col(0, u, snc, coln) for u in range(2)]
    loads[3].wait()
    for c in kept:
        c.wait()
    kept = []

    size = n // 2
    pair = 2 * 4 * rows
    i = lax.broadcasted_iota(jnp.int32, (2 * pair, pair), 0)
    j = lax.broadcasted_iota(jnp.int32, (2 * pair, pair), 1)
    mask = lax.rem(i, pair) // (4 * rows) == j // (4 * rows)

    def unit(which, u, x, d, out, gn):
        for j in range(3):
            c0 = (2 * j + which) * half
            qkv[:, j * half : (j + 1) * half] = dims(x, wq[:, c0 : c0 + half], 1, 0).astype(BF16)
        t_size = size if which == 0 else pair
        base = u * size

        def one(t, _):
            r = pl.ds(pl.multiple_of(t * t_size, t_size), t_size)
            for p in range(half // LANES):
                c = p * LANES
                q, k, v = (qkv[r, j * half + c : j * half + c + LANES] for j in range(3))
                o, dq, dk, dv = attend(q, k, v, d[r, c : c + LANES], scale, mask if which else None)
                out[r, c : c + LANES] = o
                g = pl.ds(pl.multiple_of(base + t * t_size, t_size), t_size)
                for j, value in enumerate((dq, dk, dv)):
                    grads[which, g, j * half + c : j * half + c + LANES] = value
            return 0

        lax.fori_loop(0, size // t_size, one, 0)
        total = None
        for j in range(3):
            c0 = (2 * j + which) * half
            g = grads[which, base : base + size, j * half : (j + 1) * half]
            back = dims(g, wq[:, c0 : c0 + half], 1, 1)
            total = back if total is None else total + back
        gn[...] = total.astype(BF16)

    def wgrad(which, x):
        for j in range(3):
            g = grads[which, :, j * half : (j + 1) * half]
            w2[which, :, j * half : (j + 1) * half] = dims(x, g, 0, 0).astype(BF16)

    for u in range(2):
        legs.got_row(1, u, rowd)
        legs.got_row(0, u, rown)
        unit(0, u, rown[u], rowd.at[u], orow.at[u], gnr.at[u])
        kept.append(legs.home_row(2, u, orow, orow_t))
        kept.append(legs.home_row(3, u, gnr, gnr_t))
    wgrad(0, rown[...].reshape(n, width))

    @pl.when(at.core == 1)
    def _():
        weights.swap(w2.at[0]).start()

    for u in range(2):
        legs.got_col(1, u, cold)
        legs.got_col(0, u, coln)
        c4 = cols // 8
        x = coln[u * c4 : (u + 1) * c4].reshape(size, width)
        dd[...] = cold[u * c4 : (u + 1) * c4].reshape(size, half)
        unit(1, u, x, dd, oo, gg)
        ocol[u * c4 : (u + 1) * c4] = oo[...].reshape(c4, 4 * rows, half)
        gnc[u * c4 : (u + 1) * c4] = gg[...].reshape(c4, 4 * rows, width)
        kept.append(legs.home_col(2, u, ocol, ocol_t))
        kept.append(legs.home_col(3, u, gnc, gnc_t))
        if u == 0:

            @pl.when(at.core == 0)
            def _():
                weights.along_x(lambda block: w2[0, block, :].astype(F32))

    wgrad(1, coln[...].reshape(n, width))

    @pl.when(at.core == 0)
    def _():
        weights.swap(w2.at[1]).start()
        weights.scatter_yz()

    @pl.when(at.core == 1)
    def _():
        weights.along_x(lambda block: w2[1, block, :].astype(F32))

    @pl.when(at.core == 0)
    def _():
        weights.gather_yz()

    for c in kept:
        c.wait()
    for u in range(2):
        legs.back_row(2, u, orow_t)
        legs.back_col(2, u, ocol_t)
    att[:, 0:half] = orow_t[...].reshape(n, half)
    att[:, half:width] = dims(perm[...], ocol_t[...].reshape(n, half), 0, 0).astype(BF16)

    def cot_half(h):
        return cot[:, pl.ds(pl.multiple_of(h * half, LANES), half)]

    go_out[...] = dims(att[...], cot_half(1 - at.core), 0, 0).astype(BF16)
    outs.swap(go_out).start()
    go_own[...] = dims(att[...], cot_half(at.core), 0, 0)
    mixed[...] = (res[...] + dims(att[...], wo[...], 1, 0)).astype(BF16)

    @pl.when(at.core == 0)
    def _():
        weights.swap_back()

    @pl.when(at.core == 1)
    def _():
        weights.scatter_yz()

    outs.along_x(lambda block: go_own[block, :])

    @pl.when(at.core == 1)
    def _():
        weights.gather_yz()

    outs.scatter_yz()
    for u in range(2):
        legs.back_row(3, u, gnr_t)
        legs.back_col(3, u, gnc_t)
    residual = res[...]
    grad_normed = gnr_t[...].reshape(n, width).astype(F32) + dims(perm[...], gnc_t[...].reshape(n, width), 0, 0)
    inv = lax.rsqrt(jnp.mean(residual * residual, axis=-1, keepdims=True) + 1e-06)
    pre = residual * inv
    sm_gain = jnp.sum(grad_normed * pre, axis=0, keepdims=True)
    g = grad_normed * gain[...]
    grad_residual = inv * (g - pre * jnp.mean(g * pre, axis=-1, keepdims=True)) + cot[...].astype(F32)
    gf = grad_residual.astype(BF16)
    gfine[...] = gf
    coarse_row = lax.broadcasted_iota(jnp.int32, (n, 8 * part), 1)

    def dense(core):
        named = coarse_row // part * own + lax.rem(coarse_row, part) + core * part
        return dims(onehot(named == ptok[...]), gf, 0, 0)

    co_out[...] = dense(1 - at.core).astype(BF16)
    go(co_out, co_in, co_s.at[0], co_r.at[0], partner)
    levels = dims(lv[...], gf, 0, 0)[0:8]
    row = lax.broadcasted_iota(jnp.int32, (8, half), 0)
    sm_own[0] = jnp.where(row == 0, sm_gain[:, 0:half], levels[:, 0:half])
    sm_own[1] = jnp.where(row == 0, sm_gain[:, half:width], levels[:, half:width])
    for i, dev in enumerate(dp_dev):
        go(sm_own, sm_in.at[i], s1_s.at[i], s1_r.at[i], dev)
    co_own[...] = dense(at.core)
    rcopy(co_out, co_in, co_s.at[0], co_r.at[0], partner).wait_recv()
    for i, (a, b) in enumerate(FXP):
        owner = at.fx_at(a, b)
        block = pl.ds(pl.multiple_of(owner * part, part), part)
        cf_out[i] = (co_own[block, :] + co_in[block, :].astype(F32)).astype(BF16)
        go(cf_out.at[i], cf_in.at[i], cf_s.at[i], cf_r.at[i], fx_dev[i])
    total = sm_own[...]
    for i, dev in enumerate(dp_dev):
        rcopy(sm_own, sm_in.at[i], s1_s.at[i], s1_r.at[i], dev).wait_recv()
        total = total + sm_in[i]
    sm_mid[...] = total
    for i, (a, b) in enumerate(YZP):
        go(sm_mid, sm_in2.at[i], s2_s.at[i], s2_r.at[i], at.yz(a, b)[0])
    outs.gather_yz()

    @pl.when(at.core == 1)
    def _():
        weights.swap_back()

    weights.finish()
    for h in range(2):
        for j in range(3):
            for b in range(half // LANES):
                c0 = (2 * j + h) * half + b * LANES
                gq[:, c0 : c0 + LANES] = weights.block(h, j * (half // LANES) + b) * grad_scale
    block = pl.ds(pl.multiple_of(at.fx * part, part), part)
    value = co_own[block, :] + co_in[block, :].astype(F32)
    for i in range(7):
        rcopy(cf_out.at[i], cf_in.at[i], cf_s.at[i], cf_r.at[i], fx_dev[i]).wait_recv()
        value = value + cf_in[i].astype(F32)
    cy_out[...] = value.astype(BF16)
    for i, (a, c) in enumerate(FYP):
        go(cy_out, cy_in.at[i], cy_s.at[i], cy_r.at[i], fy_dev[i])
    outs.swap_back()
    total = sm_mid[...]
    for i, (a, b) in enumerate(YZP):
        rcopy(sm_mid, sm_in2.at[i], s2_s.at[i], s2_r.at[i], at.yz(a, b)[0]).wait_recv()
        total = total + sm_in2[i]
    small[...] = total * grad_scale
    for i in range(3):
        rcopy(cy_out, cy_in.at[i], cy_s.at[i], cy_r.at[i], fy_dev[i]).wait_recv()
    gcoarse[pl.ds(pl.multiple_of(at.core * part, part), part), :] = cy_out[...].astype(F32) + cy_in[1].astype(F32)
    gcoarse[pl.ds(pl.multiple_of((1 - at.core) * part, part), part), :] = cy_in[0].astype(F32) + cy_in[2].astype(F32)
    outs.finish()
    for h in range(2):
        for b in range(half // LANES):
            c0 = h * half + b * LANES
            gout[:, c0 : c0 + LANES] = outs.block(h, b) * grad_scale
    for c in sent:
        c.wait_send()
    weights.drain()
    outs.drain()


def layer(fine, cot, ptok, coarse, level, table, gain, wq, wo, rows, cols, scale, grad_scale):
    n, width = fine.shape
    half = width // 2
    own = coarse.shape[0]
    part = own // 2
    dma = pltpu.SemaphoreType.DMA
    vmem = pltpu.VMEM
    hbm = pl.BlockSpec(memory_space=pl.ANY)
    here = pl.BlockSpec(memory_space=pltpu.VMEM)
    r2, c8, c4 = rows // 8, cols * 8, cols // 4
    return pl.pallas_call(
        functools.partial(layer_kernel, rows, cols, scale, grad_scale),
        name="layer",
        out_shape=[
            jax.ShapeDtypeStruct((n, width), BF16),
            jax.ShapeDtypeStruct((n, width), BF16),
            jax.ShapeDtypeStruct((own, width), F32),
            jax.ShapeDtypeStruct((width // 4, 6 * half), F32),
            jax.ShapeDtypeStruct((width // 4, width), F32),
            jax.ShapeDtypeStruct((2, 8, half), F32),
        ],
        in_specs=[hbm, hbm, here, here, here, here, here, hbm, hbm],
        out_specs=[here] * 6,
        scratch_shapes=[
            vmem((n, width), BF16), vmem((n, width), BF16), vmem((width, 6 * half), BF16), vmem((width, width), BF16),
            vmem((8 * own, width + LANES), BF16), vmem((n, n), BF16), vmem((n, width), F32), vmem((n, LANES), BF16),
            vmem((rows, cols, width), BF16), vmem((rows, cols, half), BF16),
            vmem((cols, rows, width), BF16), vmem((cols, rows, half), BF16),
            vmem((r2, c8, width), BF16), vmem((r2, c8, half), BF16),
            vmem((c4, rows * 4, width), BF16), vmem((c4, rows * 4, half), BF16),
            vmem((n // 2, 3 * half), BF16), vmem((2, n, 3 * half), BF16), vmem((2, width, 3 * half), BF16),
            vmem((r2, c8, half), BF16), vmem((r2, c8, width), BF16),
            vmem((c4, rows * 4, half), BF16), vmem((c4, rows * 4, width), BF16),
            vmem((rows, cols, half), BF16), vmem((rows, cols, width), BF16),
            vmem((cols, rows, half), BF16), vmem((cols, rows, width), BF16),
            vmem((n // 2, half), BF16), vmem((n // 2, half), BF16), vmem((n // 2, width), BF16),
            vmem((n, width), BF16), vmem((width, half), BF16), vmem((width, half), F32),
            vmem((8 * part, width), BF16), vmem((8 * part, width), BF16), vmem((8 * part, width), F32),
            vmem((7, part, width), BF16), vmem((7, part, width), BF16),
            vmem((part, width), BF16), vmem((3, part, width), BF16),
            vmem((2, 8, half), F32), vmem((7, 2, 8, half), F32), vmem((2, 8, half), F32), vmem((15, 2, 8, half), F32),
            dma((4,)), dma((7,)), dma((7,)), dma((7,)), dma((7,)),
            dma((4, 2, 7)), dma((4, 2, 7)), dma((4, 2, 3)), dma((4, 2, 3)), dma((4, 4)),
            dma((1,)), dma((1,)), dma((7,)), dma((7,)), dma((3,)), dma((3,)),
            dma((7,)), dma((7,)), dma((15,)), dma((15,)),
            *Reduce.scratch(width // 4, 3 * half // LANES),
            *Reduce.scratch(width // 4, half // LANES),
        ],
        compiler_params=pltpu.CompilerParams(
            collective_id=0, has_side_effects=True, vmem_limit_bytes=62 << 20
        ),
    )(fine, cot, ptok, coarse, level, table, gain, wq, wo)


def local(
    fine_tokens,
    parent,
    coarse_tokens,
    tile_level,
    level_table,
    norm_gain,
    qkv_weight,
    out_weight,
    cotangent,
):
    _, rows, cols, width = fine_tokens.shape
    half = width // 2
    n = rows * cols
    own = coarse_tokens.shape[1]
    scale = (width // HEADS) ** (-0.5)
    total_tokens = n * lax.axis_size("dp") * lax.axis_size("fy") * lax.axis_size("fx")
    grad_scale = 1.0 / math.sqrt(total_tokens)
    fine = fine_tokens.reshape(n, width)
    cot = cotangent.reshape(n, width)
    ptok = jnp.broadcast_to(parent.reshape(n // BLK, 1), (n // BLK, BLK)).reshape(n, 1)
    gain = norm_gain.reshape(1, width)
    mixed, gfine, gcoarse, gq, gout, small = layer(
        fine, cot, ptok, coarse_tokens.reshape(own, width), tile_level.reshape(own, 1),
        level_table, gain, qkv_weight, out_weight, rows, cols, scale, grad_scale,
    )
    vectors = jnp.concatenate([small[0], small[1]], axis=-1)
    share = width // 4
    ggain = lax.dynamic_slice_in_dim(vectors[0], lax.axis_index("dp") * share, share)
    return (
        mixed.reshape(fine_tokens.shape),
        gfine.reshape(fine_tokens.shape),
        gcoarse[None],
        gq,
        gout,
        ggain,
        vectors[1 : 1 + LEVELS],
    )


def solution(mesh):
    return jax.shard_map(
        local,
        mesh=mesh,
        in_specs=(
            P("dp", "fy", "fx", None),
            P("dp", "fy", "fx"),
            P("dp", "fx", None),
            P("dp", "fx"),
            P(),
            P(),
            P(),
            P(),
            P("dp", "fy", "fx", None),
        ),
        out_specs=(
            P("dp", "fy", "fx", None),
            P("dp", "fy", "fx", None),
            P("dp", "fx", None),
            P("dp", None),
            P("dp", None),
            P("dp"),
            P(),
        ),
        check_vma=False,
    )
```

```python
import functools
import math

import jax
import jax.numpy as jnp
from jax import lax
from jax.experimental import pallas as pl
from jax.experimental.pallas import tpu as pltpu
from jax.sharding import PartitionSpec as P

HEADS = 12
BLK = 4
LEVELS = 3
MESH = pl.DeviceIdType.MESH
F32 = jnp.float32
BF16 = jnp.bfloat16
FXP = [(a, b) for a in range(2) for b in range(4) if (a, b) != (0, 0)]
FYP = [(0, 1), (1, 0), (1, 1)]
YZP = [(a, b) for a in range(4) for b in range(4) if (a, b) != (0, 0)]
LANES = 128
VMEM_LIMIT = 52 << 20


def dims(a, b, ca, cb):
    return lax.dot_general(a, b, (((ca,), (cb,)), ((), ())), preferred_element_type=F32)


class Place:
    def __init__(self):
        self.dp = lax.axis_index("dp")
        self.fy = lax.axis_index("fy")
        self.fx = lax.axis_index("fx")
        self.zh, self.core = self.fy // 2, self.fy % 2
        self.zl, self.y = self.fx // 4, self.fx % 4
        self.z = self.zh * 2 + self.zl

    def fx_at(self, a, b):
        return lax.rem(self.zl + a, 2) * 4 + lax.rem(self.y + b, 4)

    def fy_at(self, a, c):
        return lax.rem(self.zh + a, 2) * 2 + lax.rem(self.core + c, 2)

    def yz(self, a, b):
        z, y = lax.rem(self.z + a, 4), lax.rem(self.y + b, 4)
        dev = {"fy": (z // 2) * 2 + self.core, "fx": (z % 2) * 4 + y}
        return dev, z * 4 + y

    def dp_at(self, d):
        return lax.rem(self.dp + d, 4)


def rcopy(src, dst, ss, rs, dev):
    return pltpu.make_async_remote_copy(
        src_ref=src, dst_ref=dst, send_sem=ss, recv_sem=rs, device_id=dev, device_id_type=MESH
    )


def greet(devs):
    barrier = pltpu.get_barrier_semaphore()
    for dev in devs:
        pl.semaphore_signal(barrier, inc=1, device_id=dev, device_id_type=MESH)
    pl.semaphore_wait(barrier, len(devs))


def onehot(cond):
    return jnp.where(cond, 1.0, 0.0).astype(BF16)


def to_columns(rows, cols):
    n = rows * cols
    new = lax.broadcasted_iota(jnp.int32, (n, n), 0)
    old = lax.broadcasted_iota(jnp.int32, (n, n), 1)
    return onehot(old == lax.rem(new, rows) * cols + new // rows)


def attend(q, k, v, d, scale, mask):
    size, lanes = q.shape
    first = lax.broadcasted_iota(jnp.int32, (size, lanes), 1) < lanes // 2

    def stack(t):
        zero = jnp.zeros_like(t)
        return jnp.concatenate([jnp.where(first, t, zero), jnp.where(first, zero, t)], axis=0)

    def join(t):
        return jnp.where(first, t[:size], t[size:])

    qs = stack((q.astype(F32) * scale).astype(BF16))
    ds_ = stack(d)
    s = dims(qs, k, 1, 1)
    if mask is not None:
        s = jnp.where(mask, s, -1e30)
    e = jnp.exp(s - jnp.max(s, axis=-1, keepdims=True))
    w = e * (1.0 / jnp.sum(e, axis=-1, keepdims=True))
    wb = w.astype(BF16)
    out = join(dims(wb, v, 1, 0)).astype(BF16)
    dv = dims(wb, ds_, 0, 0).astype(BF16)
    gw = dims(ds_, v, 1, 1)
    inner = jnp.sum(w * gw, axis=-1, keepdims=True)
    gs = (w * (gw - inner)).astype(BF16)
    dq = (join(dims(gs, k, 1, 0)) * scale).astype(BF16)
    dk = dims(gs, qs, 0, 0).astype(BF16)
    return out, dq, dk, dv


class Reduce:
    @staticmethod
    def gathered(rows, nb):
        return (2, -(-(rows * nb // 16) // 16) * 256, LANES)

    @staticmethod
    def scratch(rows, nb):
        dma = pltpu.SemaphoreType.DMA
        piece = Reduce.gathered(rows, nb)[1] // 16
        return [
            pltpu.VMEM((4 * rows, nb * LANES), BF16),
            pltpu.VMEM((3, rows, nb * LANES), BF16),
            pltpu.VMEM((3, rows, nb * LANES), BF16),
            pltpu.VMEM((rows, nb * LANES), F32),
            pltpu.VMEM((16 * piece, LANES), BF16),
            pltpu.VMEM((15, piece, LANES), BF16),
            dma((2,)), dma((2,)), dma((3,)), dma((3,)), dma((15,)), dma((15,)), dma((15,)), dma((15,)),
        ]

    def __init__(self, at, ag, refs, rows, nb):
        self.ag = ag
        (self.cx, self.xs, self.xr, self.acc, self.p16, self.r16,
         self.c_s, self.c_r, self.x_s, self.x_r, self.r_s, self.r_r, self.g_s, self.g_r) = refs
        self.at, self.rows, self.nb = at, rows, nb
        self.piece = self.r16.shape[1]
        self.partner = {"fy": at.fy_at(0, 1)}

    def go(self, c):
        c.start()

    def swap(self, src):
        return rcopy(src, self.cx, self.c_s.at[0], self.c_r.at[0], self.partner)

    def drain(self):
        rcopy(self.cx, self.cx, self.c_s.at[0], self.c_r.at[0], self.partner).wait_send()
        ref = self.ag.at[self.at.core]
        rcopy(ref, ref, self.c_s.at[1], self.c_r.at[1], self.partner).wait_send()
        for d in range(3):
            rcopy(self.xs.at[d], self.xr.at[d], self.x_s.at[d], self.x_r.at[d], self.partner).wait_send()
        for i in range(15):
            ref = self.r16.at[i]
            rcopy(ref, ref, self.r_s.at[i], self.r_r.at[i], self.partner).wait_send()
            rcopy(ref, ref, self.g_s.at[i], self.g_r.at[i], self.partner).wait_send()

    def along_x(self, mine):
        self.swap(self.cx).wait_recv()
        for d in (2, 1, 3, 0):
            i = self.at.dp_at(d)
            block = pl.ds(pl.multiple_of(i * self.rows, self.rows), self.rows)
            value = mine(block) + self.cx[block, :].astype(F32)
            if d == 0:
                self.acc[...] = value
            else:
                self.xs[d - 1] = value.astype(BF16)
                self.go(rcopy(
                    self.xs.at[d - 1], self.xr.at[d - 1], self.x_s.at[d - 1], self.x_r.at[d - 1], {"dp": i}
                ))

    def scatter_yz(self):
        for d in range(3):
            rcopy(self.xs.at[d], self.xr.at[d], self.x_s.at[d], self.x_r.at[d], {"dp": self.at.dp}).wait_recv()
        rows = self.rows
        for b in range(self.nb):
            lanes = slice(b * LANES, (b + 1) * LANES)
            value = self.acc[:, lanes]
            for d in range(3):
                value = value + self.xr[d, :, lanes].astype(F32)
            self.p16[b * rows : (b + 1) * rows, :] = value.astype(BF16)
        used = self.nb * rows
        if used < self.p16.shape[0]:
            self.p16[used:, :] = jnp.zeros((self.p16.shape[0] - used, LANES), BF16)
        for i, (a, b) in enumerate(YZP):
            dev, q = self.at.yz(a, b)
            self.go(rcopy(self.p16.at[self.slot(q)], self.r16.at[i], self.r_s.at[i], self.r_r.at[i], dev))

    def slot(self, q):
        return pl.ds(pl.multiple_of(q * self.piece, self.piece), self.piece)

    def gather_yz(self):
        at = self.at
        _, q = at.yz(0, 0)
        value = self.p16[self.slot(q), :].astype(F32)
        for i in range(15):
            dev, _ = at.yz(*YZP[i])
            rcopy(self.r16.at[i], self.r16.at[i], self.r_s.at[i], self.r_r.at[i], dev).wait_recv()
            value = value + self.r16[i].astype(F32)
        self.ag[at.core, self.slot(q), :] = value.astype(BF16)
        src = self.ag.at[at.core, self.slot(q)]
        for i, (a, b) in enumerate(YZP):
            dev, _ = at.yz(a, b)
            self.go(rcopy(src, src, self.g_s.at[i], self.g_r.at[i], dev))

    def swap_back(self):
        at = self.at
        for i, (a, b) in enumerate(YZP):
            dev, q = at.yz(4 - a, 4 - b)
            ref = self.ag.at[at.core, self.slot(q)]
            rcopy(ref, ref, self.g_s.at[i], self.g_r.at[i], dev).wait_recv()
        ref = self.ag.at[at.core]
        self.go(rcopy(ref, ref, self.c_s.at[1], self.c_r.at[1], self.partner))

    def finish(self):
        ref = self.ag.at[1 - self.at.core]
        rcopy(ref, ref, self.c_s.at[1], self.c_r.at[1], self.partner).wait_recv()


class Legs:
    def __init__(self, at, rows, cols, sems):
        self.at, self.rows, self.cols = at, rows, cols
        self.row_s, self.row_r, self.col_s, self.col_r, self.loc = sems
        self.fx_dev = [{"fx": at.fx_at(a, b)} for a, b in FXP]
        self.fy_dev = [{"fy": at.fy_at(a, c)} for a, c in FYP]
        self.sent = []
        self.kept = []

    def send(self, src, dst, ss, rs, dev):
        c = rcopy(src, dst, ss, rs, dev)
        c.start()
        self.sent.append(c)

    def keep(self, src, dst, sem):
        c = pltpu.make_async_copy(src, dst, sem)
        c.start()
        return c

    def token_row(self, ref, u, owner):
        return ref.at[pl.ds(owner * 2 + u, 1)]

    def token_col(self, ref, u, owner):
        return ref.at[pl.ds(owner * (self.cols // 4) + u * (self.cols // 8), self.cols // 8)]

    def owner_row(self, ref, u, member):
        return ref.at[pl.ds(u, 1), pl.ds(member * self.cols, self.cols)]

    def owner_col(self, ref, u, member):
        return ref.at[pl.ds(u * (self.cols // 8), self.cols // 8), pl.ds(member * self.rows, self.rows)]

    def out_row(self, kind, u, src, dst):
        at = self.at
        for i, (a, b) in enumerate(FXP):
            self.send(
                self.token_row(src, u, at.fx_at(a, b)), self.owner_row(dst, u, at.fx),
                self.row_s.at[kind, u, i], self.row_r.at[kind, u, i], self.fx_dev[i],
            )
        return self.keep(self.token_row(src, u, at.fx), self.owner_row(dst, u, at.fx), self.loc.at[kind, u])

    def out_col(self, kind, u, src, dst):
        at = self.at
        for i, (a, c) in enumerate(FYP):
            self.send(
                self.token_col(src, u, at.fy_at(a, c)), self.owner_col(dst, u, at.fy),
                self.col_s.at[kind, u, i], self.col_r.at[kind, u, i], self.fy_dev[i],
            )
        return self.keep(self.token_col(src, u, at.fy), self.owner_col(dst, u, at.fy), self.loc.at[kind, 2 + u])

    def got_row(self, kind, u, dst):
        for i, (a, b) in enumerate(FXP):
            ref = self.owner_row(dst, u, self.at.fx_at(a, 4 - b))
            rcopy(ref, ref, self.row_s.at[kind, u, i], self.row_r.at[kind, u, i], self.fx_dev[i]).wait_recv()

    def got_col(self, kind, u, dst):
        for i, (a, c) in enumerate(FYP):
            ref = self.owner_col(dst, u, self.at.fy_at(a, c))
            rcopy(ref, ref, self.col_s.at[kind, u, i], self.col_r.at[kind, u, i], self.fy_dev[i]).wait_recv()

    def home_row(self, kind, u, src, dst):
        at = self.at
        for i, (a, b) in enumerate(FXP):
            self.send(
                self.owner_row(src, u, at.fx_at(a, b)), self.token_row(dst, u, at.fx),
                self.row_s.at[kind, u, i], self.row_r.at[kind, u, i], self.fx_dev[i],
            )
        return self.keep(self.owner_row(src, u, at.fx), self.token_row(dst, u, at.fx), self.loc.at[kind, u])

    def home_col(self, kind, u, src, dst):
        at = self.at
        for i, (a, c) in enumerate(FYP):
            self.send(
                self.owner_col(src, u, at.fy_at(a, c)), self.token_col(dst, u, at.fy),
                self.col_s.at[kind, u, i], self.col_r.at[kind, u, i], self.fy_dev[i],
            )
        return self.keep(self.owner_col(src, u, at.fy), self.token_col(dst, u, at.fy), self.loc.at[kind, 2 + u])

    def back_row(self, kind, u, dst):
        for i, (a, b) in enumerate(FXP):
            ref = self.token_row(dst, u, self.at.fx_at(a, 4 - b))
            rcopy(ref, ref, self.row_s.at[kind, u, i], self.row_r.at[kind, u, i], self.fx_dev[i]).wait_recv()

    def back_col(self, kind, u, dst):
        for i, (a, c) in enumerate(FYP):
            ref = self.token_col(dst, u, self.at.fy_at(a, c))
            rcopy(ref, ref, self.col_s.at[kind, u, i], self.col_r.at[kind, u, i], self.fy_dev[i]).wait_recv()


def extra_devs(at):
    return [{"fy": at.fy_at(1, 0), "fx": at.fx_at(a, b)} for a, b in FXP]


N_RED = 14


def layer_kernel(
    rows, cols, scale, fine_h, cot_h, parent, coarse, level, table, gain, wq_h, wo_h,
    mixed_h, gfine_h, gcoarse_h, wsum_h, osum_h, small_h,
    fine, cot, wq, wo, tab, perm, pick, res, lv,
    sn, sd, snc, sdc, rown, rowd, coln, cold, qkv, grads, w2,
    orow, gnr, ocol, gnc, orow_t, gnr_t, ocol_t, gnc_t, dd, oo, gg,
    att, go_out, go_own, co_out, co_in, co_own, cf_out, cf_in, cy_out, cy_in,
    sm_own, sm_in, sm_mid, sm_in2, mixed, gfine, gcoarse, wsum, osum, small,
    ld, st, ag_s, ag_r, fw_s, fw_r, row_s, row_r, col_s, col_r, loc,
    co_s, co_r, cf_s, cf_r, cy_s, cy_r, s1_s, s1_r, s2_s, s2_r, *red,
):
    at = Place()
    n, width = fine.shape
    half = width // 2
    own = coarse.shape[0]
    part = own // 2
    halfway = part * 8
    legs = Legs(at, rows, cols, (row_s, row_r, col_s, col_r, loc))
    fx_dev, fy_dev = legs.fx_dev, legs.fy_dev
    partner = fy_dev[0]
    dp_off = [(d, c) for d in range(4) for c in range(2) if (d, c) != (0, 0)]
    dp_dev = [{"dp": at.dp_at(d), "fy": at.fy_at(0, c)} for d, c in dp_off]
    weights = Reduce(at, wsum, red[:N_RED], width // 4, 3 * half // LANES)
    outs = Reduce(at, osum, red[N_RED:], width // 4, half // LANES)
    sent = legs.sent
    go = legs.send
    stores = []

    def store(src, dst):
        c = pltpu.make_async_copy(src, dst, st.at[len(stores)])
        c.start()
        stores.append(c)

    loads = [
        pltpu.make_async_copy(a, b, ld.at[i])
        for i, (a, b) in enumerate(((cot_h, cot), (wo_h, wo), (fine_h, fine), (wq_h, wq)))
    ]
    for c in loads:
        c.start()
    as_row = onehot(lax.broadcasted_iota(jnp.int32, (8, own), 0) == level[...] + 1)
    same = lax.broadcasted_iota(jnp.int32, (8, LANES), 0) == lax.broadcasted_iota(jnp.int32, (8, LANES), 1)
    lev = dims(as_row, onehot(same), 0, 0)
    add = jnp.where(lev[:, 1:2] > 0.5, table[0:1, :], jnp.where(lev[:, 2:3] > 0.5, table[1:2, :], table[2:3, :]))
    summary = (coarse[...].astype(F32) + add).astype(BF16)
    for h in range(2):
        mine = pl.ds(h * halfway + at.fx * part, part)
        tab[mine, 0:width] = summary[h * part : (h + 1) * part]
        tab[mine, width : width + LANES] = lev[h * part : (h + 1) * part].astype(BF16)
    greet(fx_dev + fy_dev[1:] + extra_devs(at) + dp_dev)

    def chunk(owner, core):
        return tab.at[pl.ds(core * halfway + owner * part, part)]

    def across(a, b):
        fx = at.fx_at(a, b)
        return {"fx": fx} if a == 0 else {"fx": fx, "fy": at.fy_at(at.core, 0)}

    for i, (a, b) in enumerate(FXP):
        go(chunk(at.fx, at.core), chunk(at.fx, at.core), ag_s.at[i], ag_r.at[i], across(a, b))
    perm[...] = to_columns(rows, cols)
    p = parent[0]
    p = lax.rem(p, own) // part * halfway + p // own * part + lax.rem(p, part)
    token = lax.broadcasted_iota(jnp.int32, (n, rows), 0)
    spread = onehot(token // cols == lax.broadcasted_iota(jnp.int32, (n, rows), 1))
    high = dims(spread, (p // 16).astype(F32).astype(BF16), 1, 0)
    low = dims(spread, lax.rem(p, 16).astype(F32).astype(BF16), 1, 0)
    token = lax.broadcasted_iota(jnp.int32, high.shape, 0)
    reads = lax.rem(token, cols) // BLK == lax.broadcasted_iota(jnp.int32, high.shape, 1)
    ptok = jnp.sum(jnp.where(reads, high * 16.0 + low, 0.0), axis=-1, keepdims=True)
    pick[...] = onehot(lax.broadcasted_iota(jnp.int32, (n, n), 1).astype(F32) == ptok)
    loads[0].wait()
    loads[1].wait()
    d = dims(cot[...], wo[...], 1, 1).astype(BF16)
    sd[...] = d[:, 0:half].reshape(rows, cols, half)
    kept = [legs.out_row(1, u, sd, rowd) for u in range(2)]
    sdc[...] = dims(perm[...], d[:, half:width], 1, 0).astype(BF16).reshape(cols, rows, half)
    kept += [legs.out_col(1, u, sdc, cold) for u in range(2)]
    for i, (a, b) in enumerate(FXP):
        src = chunk(at.fx_at(a, 4 - b), at.core)
        rcopy(src, src, ag_s.at[i], ag_r.at[i], across(a, b)).wait_recv()
        go(src, src, fw_s.at[i], fw_r.at[i], partner)
    loads[2].wait()
    for i, (a, b) in enumerate(FXP):
        src = chunk(at.fx_at(a, 4 - b), 1 - at.core)
        rcopy(src, src, fw_s.at[i], fw_r.at[i], partner).wait_recv()
    read = dims(pick[...], tab[...], 1, 0)
    lv[...] = read[:, width : width + LANES].astype(BF16)
    residual = fine[...].astype(F32) + read[:, 0:width]
    res[...] = residual
    inv = lax.rsqrt(jnp.mean(residual * residual, axis=-1, keepdims=True) + 1e-06)
    normed = (residual * inv * gain[...].reshape(1, width)).astype(BF16)
    sn[...] = normed.reshape(rows, cols, width)
    kept += [legs.out_row(0, u, sn, rown) for u in range(2)]
    snc[...] = dims(perm[...], normed, 1, 0).astype(BF16).reshape(cols, rows, width)
    kept += [legs.out_col(0, u, snc, coln) for u in range(2)]
    loads[3].wait()
    for c in kept:
        c.wait()
    kept = []

    size = n // 2
    pair = 2 * 4 * rows
    i = lax.broadcasted_iota(jnp.int32, (2 * pair, pair), 0)
    j = lax.broadcasted_iota(jnp.int32, (2 * pair, pair), 1)
    mask = lax.rem(i, pair) // (4 * rows) == j // (4 * rows)

    def unit(which, u, x, d, out, gn):
        for j in range(3):
            c0 = (2 * j + which) * half
            qkv[:, j * half : (j + 1) * half] = dims(x, wq[:, c0 : c0 + half], 1, 0).astype(BF16)
        t_size = size if which == 0 else pair
        base = u * size

        def one(t, _):
            r = pl.ds(pl.multiple_of(t * t_size, t_size), t_size)
            for p in range(half // LANES):
                c = p * LANES
                q, k, v = (qkv[r, j * half + c : j * half + c + LANES] for j in range(3))
                o, dq, dk, dv = attend(q, k, v, d[r, c : c + LANES], scale, mask if which else None)
                out[r, c : c + LANES] = o
                g = pl.ds(pl.multiple_of(base + t * t_size, t_size), t_size)
                for j, value in enumerate((dq, dk, dv)):
                    grads[which, g, j * half + c : j * half + c + LANES] = value
            return 0

        lax.fori_loop(0, size // t_size, one, 0)
        total = None
        for j in range(3):
            c0 = (2 * j + which) * half
            g = grads[which, base : base + size, j * half : (j + 1) * half]
            back = dims(g, wq[:, c0 : c0 + half], 1, 1)
            total = back if total is None else total + back
        gn[...] = total.astype(BF16)

    def wgrad(which, x):
        for j in range(3):
            g = grads[which, :, j * half : (j + 1) * half]
            w2[which, :, j * half : (j + 1) * half] = dims(x, g, 0, 0).astype(BF16)

    for u in range(2):
        legs.got_row(1, u, rowd)
        legs.got_row(0, u, rown)
        unit(0, u, rown[u], rowd.at[u], orow.at[u], gnr.at[u])
        kept.append(legs.home_row(2, u, orow, orow_t))
        kept.append(legs.home_row(3, u, gnr, gnr_t))
    wgrad(0, rown[...].reshape(n, width))

    @pl.when(at.core == 1)
    def _():
        weights.swap(w2.at[0]).start()

    for u in range(2):
        legs.got_col(1, u, cold)
        legs.got_col(0, u, coln)
        c4 = cols // 8
        x = coln[u * c4 : (u + 1) * c4].reshape(size, width)
        dd[...] = cold[u * c4 : (u + 1) * c4].reshape(size, half)
        unit(1, u, x, dd, oo, gg)
        ocol[u * c4 : (u + 1) * c4] = oo[...].reshape(c4, 4 * rows, half)
        gnc[u * c4 : (u + 1) * c4] = gg[...].reshape(c4, 4 * rows, width)
        kept.append(legs.home_col(2, u, ocol, ocol_t))
        kept.append(legs.home_col(3, u, gnc, gnc_t))
        if u == 0:

            @pl.when(at.core == 0)
            def _():
                weights.along_x(lambda block: w2[0, block, :].astype(F32))

    wgrad(1, coln[...].reshape(n, width))

    @pl.when(at.core == 0)
    def _():
        weights.swap(w2.at[1]).start()
        weights.scatter_yz()

    @pl.when(at.core == 1)
    def _():
        weights.along_x(lambda block: w2[1, block, :].astype(F32))

    for c in kept:
        c.wait()
    for u in range(2):
        legs.back_row(2, u, orow_t)
        legs.back_col(2, u, ocol_t)
    att[:, 0:half] = orow_t[...].reshape(n, half)
    att[:, half:width] = dims(perm[...], ocol_t[...].reshape(n, half), 0, 0).astype(BF16)

    def cot_half(h):
        return cot[:, pl.ds(pl.multiple_of(h * half, LANES), half)]

    go_out[...] = dims(att[...], cot_half(1 - at.core), 0, 0).astype(BF16)
    outs.swap(go_out).start()
    go_own[...] = dims(att[...], cot_half(at.core), 0, 0)
    mixed[...] = (res[...] + dims(att[...], wo[...], 1, 0)).astype(BF16)

    store(mixed, mixed_h)
    outs.along_x(lambda block: go_own[block, :])
    for u in range(2):
        legs.back_row(3, u, gnr_t)
        legs.back_col(3, u, gnc_t)
    residual = res[...]
    grad_normed = gnr_t[...].reshape(n, width).astype(F32) + dims(perm[...], gnc_t[...].reshape(n, width), 0, 0)
    inv = lax.rsqrt(jnp.mean(residual * residual, axis=-1, keepdims=True) + 1e-06)
    pre = residual * inv
    sm_gain = jnp.sum(grad_normed * pre, axis=0, keepdims=True)
    g = grad_normed * gain[...].reshape(1, width)
    grad_residual = inv * (g - pre * jnp.mean(g * pre, axis=-1, keepdims=True)) + cot[...].astype(F32)
    gf = grad_residual.astype(BF16)
    gfine[...] = gf

    def dense(core):
        return dims(pick[:, pl.ds(pl.multiple_of(core * halfway, LANES), halfway)], gfine[...], 0, 0)

    co_out[...] = dense(1 - at.core).astype(BF16)
    go(co_out, co_in, co_s.at[0], co_r.at[0], partner)
    levels = dims(lv[...], gfine[...], 0, 0)[0:8]
    row = lax.broadcasted_iota(jnp.int32, (8, half), 0)
    for h in range(2):
        c = h * half
        both = jnp.where(row == 0, sm_gain[:, c : c + half], levels[:, c : c + half])
        sm_own[4 * h : 4 * h + 4, :] = both[0:4]
    for i, dev in enumerate(dp_dev):
        go(sm_own, sm_in.at[i], s1_s.at[i], s1_r.at[i], dev)
    co_own[...] = dense(at.core)
    store(gfine, gfine_h)

    @pl.when(at.core == 0)
    def _():
        weights.gather_yz()

    rcopy(co_out, co_in, co_s.at[0], co_r.at[0], partner).wait_recv()
    for i, (a, b) in enumerate(FXP):
        owner = at.fx_at(a, b)
        block = pl.ds(pl.multiple_of(owner * part, part), part)
        cf_out[i] = (co_own[block, :] + co_in[block, :].astype(F32)).astype(BF16)
        go(cf_out.at[i], cf_in.at[i], cf_s.at[i], cf_r.at[i], fx_dev[i])

    @pl.when(at.core == 1)
    def _():
        weights.scatter_yz()

    outs.scatter_yz()
    total = sm_own[...]
    for i, dev in enumerate(dp_dev):
        rcopy(sm_own, sm_in.at[i], s1_s.at[i], s1_r.at[i], dev).wait_recv()
        total = total + sm_in[i]
    sm_mid[...] = total
    for i, (a, b) in enumerate(YZP):
        go(sm_mid, sm_in2.at[i], s2_s.at[i], s2_r.at[i], at.yz(a, b)[0])

    @pl.when(at.core == 0)
    def _():
        weights.swap_back()

    block = pl.ds(pl.multiple_of(at.fx * part, part), part)
    value = co_own[block, :] + co_in[block, :].astype(F32)
    for i in range(7):
        rcopy(cf_out.at[i], cf_in.at[i], cf_s.at[i], cf_r.at[i], fx_dev[i]).wait_recv()
        value = value + cf_in[i].astype(F32)
    cy_out[...] = value.astype(BF16)
    for i, (a, c) in enumerate(FYP):
        go(cy_out, cy_in.at[i], cy_s.at[i], cy_r.at[i], fy_dev[i])

    @pl.when(at.core == 1)
    def _():
        weights.gather_yz()

    outs.gather_yz()
    total = sm_mid[...]
    for i, (a, b) in enumerate(YZP):
        rcopy(sm_mid, sm_in2.at[i], s2_s.at[i], s2_r.at[i], at.yz(a, b)[0]).wait_recv()
        total = total + sm_in2[i]
    small[...] = total
    store(small, small_h)
    for i in range(3):
        rcopy(cy_out, cy_in.at[i], cy_s.at[i], cy_r.at[i], fy_dev[i]).wait_recv()
    gcoarse[pl.ds(pl.multiple_of(at.core * part, part), part), :] = cy_out[...].astype(F32) + cy_in[1].astype(F32)
    gcoarse[pl.ds(pl.multiple_of((1 - at.core) * part, part), part), :] = cy_in[0].astype(F32) + cy_in[2].astype(F32)
    store(gcoarse, gcoarse_h)

    @pl.when(at.core == 1)
    def _():
        weights.swap_back()

    outs.swap_back()
    weights.finish()
    store(wsum, wsum_h)
    outs.finish()
    store(osum, osum_h)
    for c in sent:
        c.wait_send()
    weights.drain()
    outs.drain()
    for c in stores:
        c.wait()


def layer(fine, cot, parent, coarse, level, table, gain, wq, wo, rows, cols, scale):
    n, width = fine.shape
    half = width // 2
    own = coarse.shape[0]
    part = own // 2
    dma = pltpu.SemaphoreType.DMA
    vmem = pltpu.VMEM
    hbm = pl.BlockSpec(memory_space=pl.ANY)
    here = pl.BlockSpec(memory_space=pltpu.VMEM)
    r2, c8, c4 = rows // 8, cols * 8, cols // 4
    return pl.pallas_call(
        functools.partial(layer_kernel, rows, cols, scale),
        name="layer",
        out_shape=[
            jax.ShapeDtypeStruct((n, width), BF16),
            jax.ShapeDtypeStruct((n, width), BF16),
            jax.ShapeDtypeStruct((own, width), F32),
            jax.ShapeDtypeStruct(Reduce.gathered(width // 4, 3 * half // LANES), BF16),
            jax.ShapeDtypeStruct(Reduce.gathered(width // 4, half // LANES), BF16),
            jax.ShapeDtypeStruct((8, half), F32),
        ],
        in_specs=[hbm, hbm, here, here, here, here, here, hbm, hbm],
        out_specs=[hbm] * 6,
        scratch_shapes=[
            vmem((n, width), BF16), vmem((n, width), BF16), vmem((width, 6 * half), BF16), vmem((width, width), BF16),
            vmem((8 * own, width + LANES), BF16), vmem((n, n), BF16), vmem((n, n), BF16), vmem((n, width), F32), vmem((n, LANES), BF16),
            vmem((rows, cols, width), BF16), vmem((rows, cols, half), BF16),
            vmem((cols, rows, width), BF16), vmem((cols, rows, half), BF16),
            vmem((r2, c8, width), BF16), vmem((r2, c8, half), BF16),
            vmem((c4, rows * 4, width), BF16), vmem((c4, rows * 4, half), BF16),
            vmem((n // 2, 3 * half), BF16), vmem((2, n, 3 * half), BF16), vmem((2, width, 3 * half), BF16),
            vmem((r2, c8, half), BF16), vmem((r2, c8, width), BF16),
            vmem((c4, rows * 4, half), BF16), vmem((c4, rows * 4, width), BF16),
            vmem((rows, cols, half), BF16), vmem((rows, cols, width), BF16),
            vmem((cols, rows, half), BF16), vmem((cols, rows, width), BF16),
            vmem((n // 2, half), BF16), vmem((n // 2, half), BF16), vmem((n // 2, width), BF16),
            vmem((n, width), BF16), vmem((width, half), BF16), vmem((width, half), F32),
            vmem((8 * part, width), BF16), vmem((8 * part, width), BF16), vmem((8 * part, width), F32),
            vmem((7, part, width), BF16), vmem((7, part, width), BF16),
            vmem((part, width), BF16), vmem((3, part, width), BF16),
            vmem((8, half), F32), vmem((7, 8, half), F32), vmem((8, half), F32), vmem((15, 8, half), F32),
            vmem((n, width), BF16), vmem((n, width), BF16), vmem((own, width), F32),
            vmem(Reduce.gathered(width // 4, 3 * half // LANES), BF16),
            vmem(Reduce.gathered(width // 4, half // LANES), BF16), vmem((8, half), F32),
            dma((4,)), dma((6,)), dma((7,)), dma((7,)), dma((7,)), dma((7,)),
            dma((4, 2, 7)), dma((4, 2, 7)), dma((4, 2, 3)), dma((4, 2, 3)), dma((4, 4)),
            dma((1,)), dma((1,)), dma((7,)), dma((7,)), dma((3,)), dma((3,)),
            dma((7,)), dma((7,)), dma((15,)), dma((15,)),
            *Reduce.scratch(width // 4, 3 * half // LANES),
            *Reduce.scratch(width // 4, half // LANES),
        ],
        compiler_params=pltpu.CompilerParams(
            collective_id=0, has_side_effects=True, vmem_limit_bytes=VMEM_LIMIT
        ),
    )(fine, cot, parent, coarse, level, table, gain, wq, wo)


def emit_kernel(rows, grad_scale, mixed, gfine, gcoarse, wsum, osum, small, mixed_o, gfine_o, gcoarse_o, gq, gout, ggain, glevel):
    mixed_o[...] = mixed[...]
    gfine_o[...] = gfine[...]
    gcoarse_o[...] = gcoarse[...]
    half = small.shape[1]
    nb = half // LANES
    for h in range(2):
        for j in range(3):
            for b in range(nb):
                c = (2 * j + h) * half + b * LANES
                k = (j * nb + b) * rows
                gq[:, c : c + LANES] = wsum[h, k : k + rows, :].astype(F32) * grad_scale
        for b in range(nb):
            c = h * half + b * LANES
            gout[:, c : c + LANES] = osum[h, b * rows : (b + 1) * rows, :].astype(F32) * grad_scale
        glevel[:, h * half : (h + 1) * half] = small[4 * h + 1 : 4 * h + 4, :] * grad_scale
    dp = lax.axis_index("dp")
    vector = jnp.concatenate([small[0:1, :], small[4:5, :]], axis=1) * grad_scale
    share = vector[:, 0:rows]
    for i in range(1, 4):
        share = jnp.where(dp == i, vector[:, i * rows : (i + 1) * rows], share)
    ggain[...] = share


def emit(parts, grad_scale):
    mixed, gfine, gcoarse, wsum, osum, small = parts
    n, width = mixed.shape
    rows = width // 4
    here = pl.BlockSpec(memory_space=pltpu.VMEM)
    return pl.pallas_call(
        functools.partial(emit_kernel, rows, grad_scale),
        name="emit",
        out_shape=[
            jax.ShapeDtypeStruct(mixed.shape, BF16),
            jax.ShapeDtypeStruct(gfine.shape, BF16),
            jax.ShapeDtypeStruct(gcoarse.shape, F32),
            jax.ShapeDtypeStruct((rows, 3 * width), F32),
            jax.ShapeDtypeStruct((rows, width), F32),
            jax.ShapeDtypeStruct((1, rows), F32),
            jax.ShapeDtypeStruct((LEVELS, width), F32),
        ],
        in_specs=[here] * 6,
        out_specs=[here] * 7,
        compiler_params=pltpu.CompilerParams(vmem_limit_bytes=24 << 20),
    )(*parts)


def local(
    fine_tokens,
    parent,
    coarse_tokens,
    tile_level,
    level_table,
    norm_gain,
    qkv_weight,
    out_weight,
    cotangent,
):
    _, rows, cols, width = fine_tokens.shape
    half = width // 2
    n = rows * cols
    own = coarse_tokens.shape[1]
    scale = (width // HEADS) ** (-0.5)
    total_tokens = n * lax.axis_size("dp") * lax.axis_size("fy") * lax.axis_size("fx")
    grad_scale = 1.0 / math.sqrt(total_tokens)
    fine = fine_tokens.reshape(n, width)
    cot = cotangent.reshape(n, width)
    parts = layer(
        fine, cot, parent, coarse_tokens.reshape(own, width), tile_level,
        level_table, norm_gain, qkv_weight, out_weight, rows, cols, scale,
    )
    mixed, gfine, gcoarse, gq, gout, ggain, glevel = emit(parts, grad_scale)
    return (
        mixed.reshape(fine_tokens.shape),
        gfine.reshape(fine_tokens.shape),
        gcoarse[None],
        gq,
        gout,
        ggain.reshape(-1),
        glevel,
    )


def solution(mesh):
    return jax.shard_map(
        local,
        mesh=mesh,
        in_specs=(
            P("dp", "fy", "fx", None),
            P("dp", "fy", "fx"),
            P("dp", "fx", None),
            P("dp", "fx"),
            P(),
            P(),
            P(),
            P(),
            P("dp", "fy", "fx", None),
        ),
        out_specs=(
            P("dp", "fy", "fx", None),
            P("dp", "fy", "fx", None),
            P("dp", "fx", None),
            P("dp", None),
            P("dp", None),
            P("dp"),
            P(),
        ),
        check_vma=False,
    )
```

```python
import functools
import math

import jax
import jax.numpy as jnp
from jax import lax
from jax.experimental import pallas as pl
from jax.experimental.pallas import tpu as pltpu
from jax.sharding import PartitionSpec as P

HEADS = 12
BLK = 4
LEVELS = 3
MESH = pl.DeviceIdType.MESH
F32 = jnp.float32
BF16 = jnp.bfloat16
FXP = [(a, b) for a in range(2) for b in range(4) if (a, b) != (0, 0)]
FYP = [(0, 1), (1, 0), (1, 1)]
YZP = [(a, b) for a in range(4) for b in range(4) if (a, b) != (0, 0)]
LANES = 128
X_ORDER = (2, 1, 3, 0)
VMEM_LIMIT = 52 << 20


def dims(a, b, ca, cb):
    return lax.dot_general(a, b, (((ca,), (cb,)), ((), ())), preferred_element_type=F32)


class Place:
    def __init__(self):
        self.dp = lax.axis_index("dp")
        self.fy = lax.axis_index("fy")
        self.fx = lax.axis_index("fx")
        self.zh, self.core = self.fy // 2, self.fy % 2
        self.zl, self.y = self.fx // 4, self.fx % 4
        self.z = self.zh * 2 + self.zl

    def fx_at(self, a, b):
        return lax.rem(self.zl + a, 2) * 4 + lax.rem(self.y + b, 4)

    def fy_at(self, a, c):
        return lax.rem(self.zh + a, 2) * 2 + lax.rem(self.core + c, 2)

    def yz(self, a, b):
        z, y = lax.rem(self.z + a, 4), lax.rem(self.y + b, 4)
        dev = {"fy": (z // 2) * 2 + self.core, "fx": (z % 2) * 4 + y}
        return dev, y * 4 + z

    def dp_at(self, d):
        return lax.rem(self.dp + d, 4)


def rcopy(src, dst, ss, rs, dev):
    return pltpu.make_async_remote_copy(
        src_ref=src, dst_ref=dst, send_sem=ss, recv_sem=rs, device_id=dev, device_id_type=MESH
    )


def greet(devs):
    barrier = pltpu.get_barrier_semaphore()
    for dev in devs:
        pl.semaphore_signal(barrier, inc=1, device_id=dev, device_id_type=MESH)
    pl.semaphore_wait(barrier, len(devs))


def onehot(cond):
    return jnp.where(cond, 1.0, 0.0).astype(BF16)


def to_columns(rows, cols):
    n = rows * cols
    new = lax.broadcasted_iota(jnp.int32, (n, n), 0)
    old = lax.broadcasted_iota(jnp.int32, (n, n), 1)
    return onehot(old == lax.rem(new, rows) * cols + new // rows)


def attend(q, k, v, d, scale, mask):
    size, lanes = q.shape
    first = lax.broadcasted_iota(jnp.int32, (size, lanes), 1) < lanes // 2

    def stack(t):
        zero = jnp.zeros_like(t)
        return jnp.concatenate([jnp.where(first, t, zero), jnp.where(first, zero, t)], axis=0)

    def join(t):
        return jnp.where(first, t[:size], t[size:])

    qs = stack((q.astype(F32) * scale).astype(BF16))
    ds_ = stack(d)
    s = dims(qs, k, 1, 1)
    if mask is not None:
        s = jnp.where(mask, s, -1e30)
    e = jnp.exp(s - jnp.max(s, axis=-1, keepdims=True))
    w = e * (1.0 / jnp.sum(e, axis=-1, keepdims=True))
    wb = w.astype(BF16)
    out = join(dims(wb, v, 1, 0)).astype(BF16)
    dv = dims(wb, ds_, 0, 0).astype(BF16)
    gw = dims(ds_, v, 1, 1)
    inner = jnp.sum(w * gw, axis=-1, keepdims=True)
    gs = (w * (gw - inner)).astype(BF16)
    dq = (join(dims(gs, k, 1, 0)) * scale).astype(BF16)
    dk = dims(gs, qs, 0, 0).astype(BF16)
    return out, dq, dk, dv


class Reduce:
    @staticmethod
    def gathered(rows, nb):
        return (2, -(-(rows * nb // 16) // 16) * 256, LANES)

    @staticmethod
    def scratch(rows, nb):
        dma = pltpu.SemaphoreType.DMA
        piece = Reduce.gathered(rows, nb)[1] // 16
        return [
            pltpu.VMEM((4 * rows, nb * LANES), BF16),
            pltpu.VMEM((3, rows, nb * LANES), BF16),
            pltpu.VMEM((3, rows, nb * LANES), BF16),
            pltpu.VMEM((rows, nb * LANES), F32),
            pltpu.VMEM((16 * piece, LANES), BF16),
            pltpu.VMEM((3, 4 * piece, LANES), BF16),
            pltpu.VMEM((4 * piece, LANES), BF16),
            pltpu.VMEM((3, piece, LANES), BF16),
            dma((2,)), dma((5,)), dma((1,)), dma((1,)), dma((2,)), dma((2,)), dma((2,)), dma((2,)),
        ]

    def __init__(self, at, ag, refs, rows, nb):
        self.ag = ag
        (self.cx, self.xs, self.xr, self.acc, self.p16, self.ry, self.py, self.rz,
         self.c_s, self.c_r, self.x_s, self.x_r, self.r_s, self.r_r, self.g_s, self.g_r) = refs
        self.at, self.rows, self.nb = at, rows, nb
        self.piece = self.rz.shape[1]
        self.partner = {"fy": at.fy_at(0, 1)}

    def go(self, c):
        c.start()

    def x_block(self, d):
        return pl.ds(pl.multiple_of(self.at.dp_at(d) * self.rows, self.rows), self.rows)

    def swap_block(self, src, d):
        rows = self.x_block(d)
        return rcopy(src.at[rows], self.cx.at[rows], self.c_s.at[0], self.c_r.at[d], self.partner)

    def swap(self, src):
        for d in X_ORDER:
            self.swap_block(src, d).start()

    def along_x(self, mine, order=X_ORDER):
        for d in order:
            self.swap_block(self.cx, d).wait_recv()
            i = self.at.dp_at(d)
            block = self.x_block(d)
            value = mine(block) + self.cx[block, :].astype(F32)
            if d == 0:
                self.acc[...] = value
            else:
                self.xs[d - 1] = value.astype(BF16)
                rcopy(self.xs.at[d - 1], self.xr.at[d - 1], self.x_s.at[0], self.x_r.at[0], {"dp": i}).start()


    def ahead(self, z_first, k, stage):
        return self.at.yz(k, 0)[0] if z_first == (stage == 0) else self.at.yz(0, k)[0]

    def major(self, z_first):
        return self.at.z if z_first else self.at.y

    def minor(self, z_first):
        return self.at.y if z_first else self.at.z

    def column(self, z_first, k):
        size = 4 * self.piece
        return pl.ds(pl.multiple_of(lax.rem(self.major(z_first) + k, 4) * size, size), size)

    def slot(self, q):
        return pl.ds(pl.multiple_of(q * self.piece, self.piece), self.piece)

    def scatter(self, z_first):
        rcopy(self.xs, self.xr, self.x_s.at[0], self.x_r.at[0], self.partner).wait_recv()
        rows = self.rows
        for b in range(self.nb):
            lanes = slice(b * LANES, (b + 1) * LANES)
            value = self.acc[:, lanes]
            for d in range(3):
                value = value + self.xr[d, :, lanes].astype(F32)
            self.p16[b * rows : (b + 1) * rows, :] = value.astype(BF16)
        used = self.nb * rows
        if used < self.p16.shape[0]:
            self.p16[used:, :] = jnp.zeros((self.p16.shape[0] - used, LANES), BF16)
        for k in range(1, 4):
            src = self.p16.at[self.column(z_first, k)]
            rcopy(src, self.ry.at[k - 1], self.r_s.at[0], self.r_r.at[0], self.ahead(z_first, k, 0)).start()

    def scatter_again(self, z_first):
        rcopy(self.ry, self.ry, self.r_s.at[0], self.r_r.at[0], self.partner).wait_recv()
        value = self.p16[self.column(z_first, 0), :].astype(F32)
        for i in range(3):
            value = value + self.ry[i].astype(F32)
        self.py[...] = value.astype(BF16)
        for k in range(1, 4):
            src = self.py.at[self.slot(lax.rem(self.minor(z_first) + k, 4))]
            rcopy(src, self.rz.at[k - 1], self.r_s.at[1], self.r_r.at[1], self.ahead(z_first, k, 1)).start()

    def gather(self, z_first):
        at = self.at
        rcopy(self.rz, self.rz, self.r_s.at[1], self.r_r.at[1], self.partner).wait_recv()
        value = self.py[self.slot(self.minor(z_first)), :].astype(F32)
        for i in range(3):
            value = value + self.rz[i].astype(F32)
        mine = self.slot(self.major(z_first) * 4 + self.minor(z_first))
        self.ag[at.core, mine, :] = value.astype(BF16)
        src = self.ag.at[at.core, mine]
        for k in range(1, 4):
            rcopy(src, src, self.g_s.at[0], self.g_r.at[0], self.ahead(z_first, k, 1)).start()

    def pieces(self, stage):
        size = 3 * self.piece * (4 if stage else 1)
        ref = self.ag.at[self.at.core, pl.ds(0, size)]
        return rcopy(ref, ref, self.g_s.at[stage], self.g_r.at[stage], self.partner)

    def gather_again(self, z_first):
        self.pieces(0).wait_recv()
        src = self.ag.at[self.at.core, self.column(z_first, 0)]
        for k in range(1, 4):
            rcopy(src, src, self.g_s.at[1], self.g_r.at[1], self.ahead(z_first, k, 0)).start()

    def swap_back(self):
        self.pieces(1).wait_recv()
        ref = self.ag.at[self.at.core]
        rcopy(ref, ref, self.c_s.at[1], self.c_r.at[4], self.partner).start()

    def finish(self):
        ref = self.ag.at[1 - self.at.core]
        rcopy(ref, ref, self.c_s.at[1], self.c_r.at[4], self.partner).wait_recv()

    def drain(self):
        rcopy(self.cx, self.cx, self.c_s.at[0], self.c_r.at[0], self.partner).wait_send()
        rcopy(self.xs, self.xr, self.x_s.at[0], self.x_r.at[0], self.partner).wait_send()
        rcopy(self.ry, self.ry, self.r_s.at[0], self.r_r.at[0], self.partner).wait_send()
        rcopy(self.rz, self.rz, self.r_s.at[1], self.r_r.at[1], self.partner).wait_send()
        self.pieces(0).wait_send()
        self.pieces(1).wait_send()
        ref = self.ag.at[self.at.core]
        rcopy(ref, ref, self.c_s.at[1], self.c_r.at[4], self.partner).wait_send()


class Legs:
    def __init__(self, at, rows, cols, sems):
        self.at, self.rows, self.cols = at, rows, cols
        self.row_s, self.row_r, self.col_s, self.col_r, self.loc = sems
        self.fx_dev = [{"fx": at.fx_at(a, b)} for a, b in FXP]
        self.fy_dev = [{"fy": at.fy_at(a, c)} for a, c in FYP]
        self.sent = []
        self.kept = []

    def gone(self, ref, ss, rs):
        self.sent.append(rcopy(ref, ref, ss, rs, self.fx_dev[0]))

    def keep(self, src, dst, sem):
        c = pltpu.make_async_copy(src, dst, sem)
        c.start()
        self.kept.append(c)

    def token_row(self, ref, u, owner):
        return ref.at[pl.ds(owner * 2 + u, 1)]

    def token_col(self, ref, u, owner):
        return ref.at[pl.ds(owner * (self.cols // 4) + u * (self.cols // 8), self.cols // 8)]

    def owner_row(self, ref, u, member):
        return ref.at[pl.ds(u, 1), pl.ds(member * self.cols, self.cols)]

    def owner_col(self, ref, u, member):
        return ref.at[pl.ds(u * (self.cols // 8), self.cols // 8), pl.ds(member * self.rows, self.rows)]

    def tokens_row(self, ref):
        return ref.at[pl.ds(0, 7)]

    def tokens_col(self, ref):
        return ref.at[pl.ds(0, 3 * (self.cols // 8))]

    def owners_row(self, ref, u):
        return ref.at[pl.ds(u, 1), pl.ds(0, 7 * self.cols)]

    def owners_col(self, ref, u):
        return ref.at[pl.ds(u * (self.cols // 8), self.cols // 8), pl.ds(0, 3 * self.rows)]

    def out_row(self, kind, u, src, dst):
        at, ss, rs = self.at, self.row_s.at[kind, u], self.row_r.at[kind, u]
        for i, (a, b) in enumerate(FXP):
            rcopy(
                self.token_row(src, u, at.fx_at(a, b)), self.owner_row(dst, u, at.fx), ss, rs, self.fx_dev[i]
            ).start()
        self.gone(self.tokens_row(src), ss, rs)
        self.keep(self.token_row(src, u, at.fx), self.owner_row(dst, u, at.fx), self.loc.at[kind, u])

    def out_col(self, kind, u, src, dst):
        at, ss, rs = self.at, self.col_s.at[kind, u], self.col_r.at[kind, u]
        for i, (a, c) in enumerate(FYP):
            rcopy(
                self.token_col(src, u, at.fy_at(a, c)), self.owner_col(dst, u, at.fy), ss, rs, self.fy_dev[i]
            ).start()
        self.gone(self.tokens_col(src), ss, rs)
        self.keep(self.token_col(src, u, at.fy), self.owner_col(dst, u, at.fy), self.loc.at[kind, 2 + u])

    def got_row(self, kind, u, dst):
        ref = self.owners_row(dst, u)
        rcopy(ref, ref, self.row_s.at[kind, u], self.row_r.at[kind, u], self.fx_dev[0]).wait_recv()

    def got_col(self, kind, u, dst):
        ref = self.owners_col(dst, u)
        rcopy(ref, ref, self.col_s.at[kind, u], self.col_r.at[kind, u], self.fx_dev[0]).wait_recv()

    def home_row(self, kind, u, src, dst):
        at, ss, rs = self.at, self.row_s.at[kind, u], self.row_r.at[kind, u]
        for i, (a, b) in enumerate(FXP):
            rcopy(
                self.owner_row(src, u, at.fx_at(a, b)), self.token_row(dst, u, at.fx), ss, rs, self.fx_dev[i]
            ).start()
        self.gone(self.owners_row(src, u), ss, rs)
        self.keep(self.owner_row(src, u, at.fx), self.token_row(dst, u, at.fx), self.loc.at[kind, u])

    def home_col(self, kind, u, src, dst):
        at, ss, rs = self.at, self.col_s.at[kind, u], self.col_r.at[kind, u]
        for i, (a, c) in enumerate(FYP):
            rcopy(
                self.owner_col(src, u, at.fy_at(a, c)), self.token_col(dst, u, at.fy), ss, rs, self.fy_dev[i]
            ).start()
        self.gone(self.owners_col(src, u), ss, rs)
        self.keep(self.owner_col(src, u, at.fy), self.token_col(dst, u, at.fy), self.loc.at[kind, 2 + u])

    def back_row(self, kind, u, dst):
        ref = self.tokens_row(dst)
        rcopy(ref, ref, self.row_s.at[kind, u], self.row_r.at[kind, u], self.fx_dev[0]).wait_recv()

    def back_col(self, kind, u, dst):
        ref = self.tokens_col(dst)
        rcopy(ref, ref, self.col_s.at[kind, u], self.col_r.at[kind, u], self.fx_dev[0]).wait_recv()

    def settle(self):
        for c in self.kept:
            c.wait()
        self.kept = []


def extra_devs(at):
    return [{"fy": at.fy_at(1, 0), "fx": at.fx_at(a, b)} for a, b in FXP]


N_RED = 16


def layer_kernel(
    rows, cols, scale, fine_h, cot_h, parent_h, coarse_h, level_h, table_h, gain_h, wq_h, wo_h,
    mixed_h, gfine_h, gcoarse_h, wsum_h, osum_h, small_h,
    parent, coarse, level, table, gain, fine, cot, wq, wo, tab, perm, pick, res, lv,
    sn, sd, snc, sdc, rown, rowd, coln, cold, qkv, grads, w2,
    orow, gnr, ocol, gnc, orow_t, gnr_t, ocol_t, gnc_t, dd, oo, gg,
    att, go_out, go_own, co_out, co_in, co_own, cf_out, cf_in, cz, cy_out, cy_in, cc_out, cc_in,
    sm_own, sm_in, sm_mid, sm_in2, mixed, gfine, gcoarse, wsum, osum, small,
    ld, st, ag_s, ag_r, fw_s, fw_r, row_s, row_r, col_s, col_r, loc,
    co_s, co_r, cf_s, cf_r, cy_s, cy_r, s1_s, s1_r, s2_s, s2_r, *red,
):
    at = Place()
    n, width = fine.shape
    half = width // 2
    own = coarse.shape[0]
    part = own // 2
    halfway = part * 8
    legs = Legs(at, rows, cols, (row_s, row_r, col_s, col_r, loc))
    fx_dev, fy_dev = legs.fx_dev, legs.fy_dev
    partner = fy_dev[0]
    dp_off = [(d, c) for d in range(4) for c in range(2) if (d, c) != (0, 0)]
    dp_dev = [{"dp": at.dp_at(d), "fy": at.fy_at(0, c)} for d, c in dp_off]
    weights = Reduce(at, wsum, red[:N_RED], width // 4, 3 * half // LANES)
    outs = Reduce(at, osum, red[N_RED:], width // 4, half // LANES)
    sent = legs.sent
    stores = []

    def store(src, dst):
        c = pltpu.make_async_copy(src, dst, st.at[len(stores)])
        c.start()
        stores.append(c)

    loads = [
        pltpu.make_async_copy(a, b, ld.at[i])
        for i, (a, b) in enumerate((
            (cot_h, cot), (wo_h, wo), (fine_h, fine), (wq_h, wq),
            (level_h, level), (table_h, table), (coarse_h, coarse), (parent_h, parent), (gain_h, gain),
        ))
    ]
    for i in (4, 5, 6, 7, 8, 0, 1, 2, 3):
        loads[i].start()
    for i in (4, 5, 6, 7, 8):
        loads[i].wait()
    as_row = onehot(lax.broadcasted_iota(jnp.int32, (8, own), 0) == level[...] + 1)
    same = lax.broadcasted_iota(jnp.int32, (8, LANES), 0) == lax.broadcasted_iota(jnp.int32, (8, LANES), 1)
    lev = dims(as_row, onehot(same), 0, 0)
    add = jnp.where(lev[:, 1:2] > 0.5, table[0:1, :], jnp.where(lev[:, 2:3] > 0.5, table[1:2, :], table[2:3, :]))
    summary = (coarse[...].astype(F32) + add).astype(BF16)
    for h in range(2):
        mine = pl.ds(h * halfway + at.fx * part, part)
        tab[mine, 0:width] = summary[h * part : (h + 1) * part]
        tab[mine, width : width + LANES] = lev[h * part : (h + 1) * part].astype(BF16)
    greet(fx_dev + fy_dev[1:] + extra_devs(at) + dp_dev)

    def chunk(owner, core):
        return tab.at[pl.ds(core * halfway + owner * part, part)]

    def across(a, b):
        fx = at.fx_at(a, b)
        return {"fx": fx} if a == 0 else {"fx": fx, "fy": at.fy_at(at.core, 0)}

    for i, (a, b) in enumerate(FXP):
        rcopy(chunk(at.fx, at.core), chunk(at.fx, at.core), ag_s.at[0], ag_r.at[i], across(a, b)).start()
    perm[...] = to_columns(rows, cols)
    p = parent[0]
    p = lax.rem(p, own) // part * halfway + p // own * part + lax.rem(p, part)
    token = lax.broadcasted_iota(jnp.int32, (n, rows), 0)
    spread = onehot(token // cols == lax.broadcasted_iota(jnp.int32, (n, rows), 1))
    high = dims(spread, (p // 16).astype(F32).astype(BF16), 1, 1)
    low = dims(spread, lax.rem(p, 16).astype(F32).astype(BF16), 1, 1)
    token = lax.broadcasted_iota(jnp.int32, high.shape, 0)
    reads = lax.rem(token, cols) // BLK == lax.broadcasted_iota(jnp.int32, high.shape, 1)
    ptok = jnp.sum(jnp.where(reads, high * 16.0 + low, 0.0), axis=-1, keepdims=True)
    pick[...] = onehot(lax.broadcasted_iota(jnp.int32, (n, n), 1).astype(F32) == ptok)
    loads[0].wait()
    loads[1].wait()
    d = dims(cot[...], wo[...], 1, 1).astype(BF16)
    sd[...] = d[:, 0:half].reshape(rows, cols, half)
    for u in range(2):
        legs.out_row(1, u, sd, rowd)
    sdc[...] = dims(perm[...], d[:, half:width], 1, 0).astype(BF16).reshape(cols, rows, half)
    for u in range(2):
        legs.out_col(1, u, sdc, cold)
    for i, (a, b) in enumerate(FXP):
        src = chunk(at.fx_at(a, 4 - b), at.core)
        rcopy(src, src, ag_s.at[0], ag_r.at[i], across(a, b)).wait_recv()
        rcopy(src, src, fw_s.at[0], fw_r.at[0], partner).start()
    loads[2].wait()
    seven = tab.at[pl.ds(0, 7 * part)]
    legs.gone(seven, ag_s.at[0], ag_r.at[0])
    legs.gone(seven, fw_s.at[0], fw_r.at[0])
    rcopy(seven, seven, fw_s.at[0], fw_r.at[0], partner).wait_recv()
    read = dims(pick[...], tab[...], 1, 0)
    lv[...] = read[:, width : width + LANES].astype(BF16)
    residual = fine[...].astype(F32) + read[:, 0:width]
    res[...] = residual
    inv = lax.rsqrt(jnp.mean(residual * residual, axis=-1, keepdims=True) + 1e-06)
    normed = (residual * inv * gain[...].reshape(1, width)).astype(BF16)
    sn[...] = normed.reshape(rows, cols, width)
    for u in range(2):
        legs.out_row(0, u, sn, rown)
    snc[...] = dims(perm[...], normed, 1, 0).astype(BF16).reshape(cols, rows, width)
    for u in range(2):
        legs.out_col(0, u, snc, coln)
    loads[3].wait()
    legs.settle()

    size = n // 2
    pair = 2 * 4 * rows
    i = lax.broadcasted_iota(jnp.int32, (2 * pair, pair), 0)
    j = lax.broadcasted_iota(jnp.int32, (2 * pair, pair), 1)
    mask = lax.rem(i, pair) // (4 * rows) == j // (4 * rows)

    def unit(which, u, x, d, out, gn, between=None):
        for j in range(3):
            c0 = (2 * j + which) * half
            qkv[:, j * half : (j + 1) * half] = dims(x, wq[:, c0 : c0 + half], 1, 0).astype(BF16)
        t_size = size if which == 0 else pair
        base = u * size

        def one(t, _):
            r = pl.ds(pl.multiple_of(t * t_size, t_size), t_size)
            for p in range(half // LANES):
                c = p * LANES
                q, k, v = (qkv[r, j * half + c : j * half + c + LANES] for j in range(3))
                o, dq, dk, dv = attend(q, k, v, d[r, c : c + LANES], scale, mask if which else None)
                out[r, c : c + LANES] = o
                g = pl.ds(pl.multiple_of(base + t * t_size, t_size), t_size)
                for j, value in enumerate((dq, dk, dv)):
                    grads[which, g, j * half + c : j * half + c + LANES] = value
            return 0

        if between is None:
            lax.fori_loop(0, size // t_size, one, 0)
        else:
            one(0, 0)
            between()
            lax.fori_loop(1, size // t_size, one, 0)
        total = None
        for j in range(3):
            c0 = (2 * j + which) * half
            g = grads[which, base : base + size, j * half : (j + 1) * half]
            back = dims(g, wq[:, c0 : c0 + half], 1, 1)
            total = back if total is None else total + back
        gn[...] = total.astype(BF16)

    def wgrad(which, x):
        for j in range(3):
            g = grads[which, :, j * half : (j + 1) * half]
            w2[which, :, j * half : (j + 1) * half] = dims(x, g, 0, 0).astype(BF16)

    for u in range(2):
        legs.got_row(1, u, rowd)
        legs.got_row(0, u, rown)
        unit(0, u, rown[u], rowd.at[u], orow.at[u], gnr.at[u])
    wgrad(0, rown[...].reshape(n, width))

    @pl.when(at.core == 1)
    def _():
        weights.swap(w2.at[0])

    for u in range(2):
        legs.got_col(1, u, cold)
        legs.got_col(0, u, coln)
        if u == 0:
            for v in range(2):
                legs.home_row(2, v, orow, orow_t)
            legs.home_row(3, 0, gnr, gnr_t)
        c4 = cols // 8
        x = coln[u * c4 : (u + 1) * c4].reshape(size, width)
        dd[...] = cold[u * c4 : (u + 1) * c4].reshape(size, half)
        def early():
            @pl.when(at.core == 0)
            def _():
                weights.along_x(lambda block: w2[0, block, :].astype(F32), X_ORDER[:2])

        unit(1, u, x, dd, oo, gg, early if u == 0 else None)
        ocol[u * c4 : (u + 1) * c4] = oo[...].reshape(c4, 4 * rows, half)
        gnc[u * c4 : (u + 1) * c4] = gg[...].reshape(c4, 4 * rows, width)
        legs.home_col(2, u, ocol, ocol_t)
        if u == 0:
            legs.home_row(3, 1, gnr, gnr_t)
        if u == 0:

            @pl.when(at.core == 0)
            def _():
                weights.along_x(lambda block: w2[0, block, :].astype(F32), X_ORDER[2:])

    wgrad(1, coln[...].reshape(n, width))
    legs.home_col(3, 0, gnc, gnc_t)


    @pl.when(at.core == 0)
    def _():
        weights.swap(w2.at[1])

    @pl.when(at.core == 0)
    def _():
        weights.scatter(False)

    @pl.when(at.core == 1)
    def _():
        weights.along_x(lambda block: w2[1, block, :].astype(F32))

    legs.home_col(3, 1, gnc, gnc_t)
    legs.settle()
    for u in range(2):
        legs.back_row(2, u, orow_t)
        legs.back_col(2, u, ocol_t)
    att[:, 0:half] = orow_t[...].reshape(n, half)
    att[:, half:width] = dims(perm[...], ocol_t[...].reshape(n, half), 0, 0).astype(BF16)

    def cot_half(h):
        return cot[:, pl.ds(pl.multiple_of(h * half, LANES), half)]

    go_out[...] = dims(att[...], cot_half(1 - at.core), 0, 0).astype(BF16)
    outs.swap(go_out)
    go_own[...] = dims(att[...], cot_half(at.core), 0, 0)
    mixed[...] = (res[...] + dims(att[...], wo[...], 1, 0)).astype(BF16)

    store(mixed, mixed_h)

    @pl.when(at.core == 0)
    def _():
        weights.scatter_again(False)

    outs.along_x(lambda block: go_own[block, :])

    @pl.when(at.core == 0)
    def _():
        weights.gather(False)

    for u in range(2):
        legs.back_row(3, u, gnr_t)
        legs.back_col(3, u, gnc_t)
    residual = res[...]
    grad_normed = gnr_t[...].reshape(n, width).astype(F32) + dims(perm[...], gnc_t[...].reshape(n, width), 0, 0)
    inv = lax.rsqrt(jnp.mean(residual * residual, axis=-1, keepdims=True) + 1e-06)
    pre = residual * inv
    sm_gain = jnp.sum(grad_normed * pre, axis=0, keepdims=True)
    g = grad_normed * gain[...].reshape(1, width)
    grad_residual = inv * (g - pre * jnp.mean(g * pre, axis=-1, keepdims=True)) + cot[...].astype(F32)
    gf = grad_residual.astype(BF16)
    gfine[...] = gf

    def dense(core):
        return dims(pick[:, pl.ds(pl.multiple_of(core * halfway, LANES), halfway)], gfine[...], 0, 0)

    co_out[...] = dense(1 - at.core).astype(BF16)
    rcopy(co_out, co_in, co_s.at[0], co_r.at[0], partner).start()
    legs.gone(co_out, co_s.at[0], co_r.at[0])
    levels = dims(lv[...], gfine[...], 0, 0)[0:8]
    row = lax.broadcasted_iota(jnp.int32, (8, half), 0)
    for h in range(2):
        c = h * half
        both = jnp.where(row == 0, sm_gain[:, c : c + half], levels[:, c : c + half])
        sm_own[4 * h : 4 * h + 4, :] = both[0:4]
    for i, dev in enumerate(dp_dev):
        rcopy(sm_own, sm_in.at[i], s1_s.at[0], s1_r.at[0], dev).start()
    co_own[...] = dense(at.core)
    store(gfine, gfine_h)

    @pl.when(at.core == 0)
    def _():
        weights.gather_again(False)

    rcopy(co_out, co_in, co_s.at[0], co_r.at[0], partner).wait_recv()

    def block(zl, y):
        return pl.ds(pl.multiple_of((zl * 4 + y) * part, part), part)

    for b in range(1, 4):
        dev, _ = at.yz(0, b)
        y = lax.rem(at.y + b, 4)
        for zl in range(2):
            rows_ = block(zl, y)
            cf_out[b - 1, zl] = (co_own[rows_, :] + co_in[rows_, :].astype(F32)).astype(BF16)
        rcopy(cf_out.at[b - 1], cf_in.at[b - 1], cf_s.at[0], cf_r.at[0], dev).start()

    @pl.when(at.core == 1)
    def _():
        weights.scatter(True)

    outs.scatter(True)
    rcopy(sm_in, sm_in, s1_s.at[0], s1_r.at[0], partner).wait_recv()
    total = sm_own[...]
    for i in range(7):
        total = total + sm_in[i]
    sm_mid[0] = total
    for i in range(3):
        dev, _ = at.yz(i + 1, 0)
        rcopy(sm_mid.at[0], sm_in2.at[0, i], s2_s.at[0], s2_r.at[0], dev).start()

    @pl.when(at.core == 1)
    def _():
        weights.scatter_again(True)

    outs.scatter_again(True)
    rcopy(cf_in, cf_in, cf_s.at[0], cf_r.at[0], partner).wait_recv()
    for zl in range(2):
        rows_ = block(zl, at.y)
        value = co_own[rows_, :] + co_in[rows_, :].astype(F32)
        for i in range(3):
            value = value + cf_in[i, zl].astype(F32)
        cz[zl] = value
        cy_out[zl] = value.astype(BF16)
    for a in range(1, 4):
        dev, _ = at.yz(a, 0)
        rcopy(cy_out.at[lax.rem(at.zl + a, 2)], cy_in.at[a - 1], cy_s.at[0], cy_r.at[0], dev).start()

    @pl.when(at.core == 0)
    def _():
        weights.swap_back()

    rcopy(sm_in2.at[0], sm_in2.at[0], s2_s.at[0], s2_r.at[0], partner).wait_recv()
    sm_mid[1] = sm_mid[0] + sm_in2[0, 0] + sm_in2[0, 1] + sm_in2[0, 2]
    for i in range(3):
        dev, _ = at.yz(0, i + 1)
        rcopy(sm_mid.at[1], sm_in2.at[1, i], s2_s.at[1], s2_r.at[1], dev).start()

    @pl.when(at.core == 1)
    def _():
        weights.gather(True)

    outs.gather(True)
    rcopy(cy_in, cy_in, cy_s.at[0], cy_r.at[0], partner).wait_recv()
    value = cz[at.zl] + cy_in[0].astype(F32) + cy_in[1].astype(F32) + cy_in[2].astype(F32)
    gcoarse[pl.ds(pl.multiple_of(at.core * part, part), part), :] = value
    cc_out[...] = value.astype(BF16)
    rcopy(cc_out, cc_in, co_s.at[1], co_r.at[1], partner).start()

    @pl.when(at.core == 1)
    def _():
        weights.gather_again(True)

    outs.gather_again(True)
    rcopy(cc_out, cc_in, co_s.at[1], co_r.at[1], partner).wait_recv()
    gcoarse[pl.ds(pl.multiple_of((1 - at.core) * part, part), part), :] = cc_in[...].astype(F32)
    store(gcoarse, gcoarse_h)
    rcopy(sm_in2.at[1], sm_in2.at[1], s2_s.at[1], s2_r.at[1], partner).wait_recv()
    small[...] = sm_mid[1] + sm_in2[1, 0] + sm_in2[1, 1] + sm_in2[1, 2]
    store(small, small_h)

    @pl.when(at.core == 1)
    def _():
        weights.swap_back()

    outs.swap_back()
    weights.finish()
    store(wsum, wsum_h)
    outs.finish()
    store(osum, osum_h)
    legs.gone(sm_in, s1_s.at[0], s1_r.at[0])
    legs.gone(cf_in, cf_s.at[0], cf_r.at[0])
    legs.gone(cy_in, cy_s.at[0], cy_r.at[0])
    legs.gone(cc_in, co_s.at[1], co_r.at[1])
    legs.gone(sm_in2.at[0], s2_s.at[0], s2_r.at[0])
    legs.gone(sm_in2.at[1], s2_s.at[1], s2_r.at[1])
    legs.settle()
    for c in sent:
        c.wait_send()
    weights.drain()
    outs.drain()
    for c in stores:
        c.wait()


def layer(fine, cot, parent, coarse, level, table, gain, wq, wo, rows, cols, scale):
    n, width = fine.shape
    half = width // 2
    own = coarse.shape[0]
    part = own // 2
    dma = pltpu.SemaphoreType.DMA
    vmem = pltpu.VMEM
    hbm = pl.BlockSpec(memory_space=pl.ANY)
    r2, c8, c4 = rows // 8, cols * 8, cols // 4
    return pl.pallas_call(
        functools.partial(layer_kernel, rows, cols, scale),
        name="layer",
        out_shape=[
            jax.ShapeDtypeStruct((n, width), BF16),
            jax.ShapeDtypeStruct((n, width), BF16),
            jax.ShapeDtypeStruct((own, width), F32),
            jax.ShapeDtypeStruct(Reduce.gathered(width // 4, 3 * half // LANES), BF16),
            jax.ShapeDtypeStruct(Reduce.gathered(width // 4, half // LANES), BF16),
            jax.ShapeDtypeStruct((8, half), F32),
        ],
        in_specs=[hbm] * 2 + [pl.BlockSpec(memory_space=pltpu.MemorySpace.HBM)] * 5 + [hbm] * 2,
        out_specs=[hbm] * 6,
        scratch_shapes=[
            vmem(parent.shape, jnp.int32), vmem((own, width), BF16), vmem(level.shape, jnp.int32),
            vmem(table.shape, F32), vmem(gain.shape, F32),
            vmem((n, width), BF16), vmem((n, width), BF16), vmem((width, 6 * half), BF16), vmem((width, width), BF16),
            vmem((8 * own, width + LANES), BF16), vmem((n, n), BF16), vmem((n, n), BF16), vmem((n, width), F32), vmem((n, LANES), BF16),
            vmem((rows, cols, width), BF16), vmem((rows, cols, half), BF16),
            vmem((cols, rows, width), BF16), vmem((cols, rows, half), BF16),
            vmem((r2, c8, width), BF16), vmem((r2, c8, half), BF16),
            vmem((c4, rows * 4, width), BF16), vmem((c4, rows * 4, half), BF16),
            vmem((n // 2, 3 * half), BF16), vmem((2, n, 3 * half), BF16), vmem((2, width, 3 * half), BF16),
            vmem((r2, c8, half), BF16), vmem((r2, c8, width), BF16),
            vmem((c4, rows * 4, half), BF16), vmem((c4, rows * 4, width), BF16),
            vmem((rows, cols, half), BF16), vmem((rows, cols, width), BF16),
            vmem((cols, rows, half), BF16), vmem((cols, rows, width), BF16),
            vmem((n // 2, half), BF16), vmem((n // 2, half), BF16), vmem((n // 2, width), BF16),
            vmem((n, width), BF16), vmem((width, half), BF16), vmem((width, half), F32),
            vmem((8 * part, width), BF16), vmem((8 * part, width), BF16), vmem((8 * part, width), F32),
            vmem((3, 2, part, width), BF16), vmem((3, 2, part, width), BF16), vmem((2, part, width), F32),
            vmem((2, part, width), BF16), vmem((3, part, width), BF16),
            vmem((part, width), BF16), vmem((part, width), BF16),
            vmem((8, half), F32), vmem((7, 8, half), F32), vmem((2, 8, half), F32), vmem((2, 3, 8, half), F32),
            vmem((n, width), BF16), vmem((n, width), BF16), vmem((own, width), F32),
            vmem(Reduce.gathered(width // 4, 3 * half // LANES), BF16),
            vmem(Reduce.gathered(width // 4, half // LANES), BF16), vmem((8, half), F32),
            dma((9,)), dma((6,)), dma((1,)), dma((7,)), dma((1,)), dma((1,)),
            dma((4, 2)), dma((4, 2)), dma((4, 2)), dma((4, 2)), dma((4, 4)),
            dma((2,)), dma((2,)), dma((1,)), dma((1,)), dma((1,)), dma((1,)),
            dma((1,)), dma((1,)), dma((2,)), dma((2,)),
            *Reduce.scratch(width // 4, 3 * half // LANES),
            *Reduce.scratch(width // 4, half // LANES),
        ],
        compiler_params=pltpu.CompilerParams(
            collective_id=0, has_side_effects=True, vmem_limit_bytes=VMEM_LIMIT
        ),
    )(fine, cot, parent, coarse, level, table, gain, wq, wo)


def emit_kernel(rows, grad_scale, mixed, gfine, gcoarse, wsum, osum, small, mixed_o, gfine_o, gcoarse_o, gq, gout, ggain, glevel):
    mixed_o[...] = mixed[...]
    gfine_o[...] = gfine[...]
    gcoarse_o[...] = gcoarse[...]
    half = small.shape[1]
    nb = half // LANES
    for h in range(2):
        for j in range(3):
            for b in range(nb):
                c = (2 * j + h) * half + b * LANES
                k = (j * nb + b) * rows
                gq[:, c : c + LANES] = wsum[h, k : k + rows, :].astype(F32) * grad_scale
        for b in range(nb):
            c = h * half + b * LANES
            gout[:, c : c + LANES] = osum[h, b * rows : (b + 1) * rows, :].astype(F32) * grad_scale
        glevel[:, h * half : (h + 1) * half] = small[4 * h + 1 : 4 * h + 4, :] * grad_scale
    dp = lax.axis_index("dp")
    vector = jnp.concatenate([small[0:1, :], small[4:5, :]], axis=1) * grad_scale
    share = vector[:, 0:rows]
    for i in range(1, 4):
        share = jnp.where(dp == i, vector[:, i * rows : (i + 1) * rows], share)
    ggain[...] = share


def emit(parts, grad_scale):
    mixed, gfine, gcoarse, wsum, osum, small = parts
    n, width = mixed.shape
    rows = width // 4
    here = pl.BlockSpec(memory_space=pltpu.VMEM)
    return pl.pallas_call(
        functools.partial(emit_kernel, rows, grad_scale),
        name="emit",
        out_shape=[
            jax.ShapeDtypeStruct(mixed.shape, BF16),
            jax.ShapeDtypeStruct(gfine.shape, BF16),
            jax.ShapeDtypeStruct(gcoarse.shape, F32),
            jax.ShapeDtypeStruct((rows, 3 * width), F32),
            jax.ShapeDtypeStruct((rows, width), F32),
            jax.ShapeDtypeStruct((1, rows), F32),
            jax.ShapeDtypeStruct((LEVELS, width), F32),
        ],
        in_specs=[here] * 6,
        out_specs=[here] * 7,
        compiler_params=pltpu.CompilerParams(vmem_limit_bytes=24 << 20),
    )(*parts)


def local(
    fine_tokens,
    parent,
    coarse_tokens,
    tile_level,
    level_table,
    norm_gain,
    qkv_weight,
    out_weight,
    cotangent,
):
    _, rows, cols, width = fine_tokens.shape
    half = width // 2
    n = rows * cols
    own = coarse_tokens.shape[1]
    scale = (width // HEADS) ** (-0.5)
    total_tokens = n * lax.axis_size("dp") * lax.axis_size("fy") * lax.axis_size("fx")
    grad_scale = 1.0 / math.sqrt(total_tokens)
    fine = fine_tokens.reshape(n, width)
    cot = cotangent.reshape(n, width)
    parts = layer(
        fine, cot, parent.swapaxes(1, 2), coarse_tokens.reshape(own, width), tile_level,
        level_table, norm_gain, qkv_weight, out_weight, rows, cols, scale,
    )
    mixed, gfine, gcoarse, gq, gout, ggain, glevel = emit(parts, grad_scale)
    return (
        mixed.reshape(fine_tokens.shape),
        gfine.reshape(fine_tokens.shape),
        gcoarse[None],
        gq,
        gout,
        ggain.reshape(-1),
        glevel,
    )


def solution(mesh):
    return jax.shard_map(
        local,
        mesh=mesh,
        in_specs=(
            P("dp", "fy", "fx", None),
            P("dp", "fy", "fx"),
            P("dp", "fx", None),
            P("dp", "fx"),
            P(),
            P(),
            P(),
            P(),
            P("dp", "fy", "fx", None),
        ),
        out_specs=(
            P("dp", "fy", "fx", None),
            P("dp", "fy", "fx", None),
            P("dp", "fx", None),
            P("dp", None),
            P("dp", None),
            P("dp"),
            P(),
        ),
        check_vma=False,
    )
```

```python
import functools
import math

import jax
import jax.numpy as jnp
from jax import lax
from jax.experimental import pallas as pl
from jax.experimental.pallas import tpu as pltpu
from jax.sharding import PartitionSpec as P

HEADS = 12
BLK = 4
LEVELS = 3
MESH = pl.DeviceIdType.MESH
F32 = jnp.float32
BF16 = jnp.bfloat16
FXP = [(a, b) for a in range(2) for b in range(4) if (a, b) != (0, 0)]
FYP = [(0, 1), (1, 0), (1, 1)]
YZP = [(a, b) for a in range(4) for b in range(4) if (a, b) != (0, 0)]
LANES = 128
X_ORDER = (2, 1, 3, 0)
VMEM_LIMIT = 67043328
EMIT_LIMIT = 67043328


def dims(a, b, ca, cb):
    return lax.dot_general(a, b, (((ca,), (cb,)), ((), ())), preferred_element_type=F32)


class Place:
    def __init__(self):
        self.dp = lax.axis_index("dp")
        self.fy = lax.axis_index("fy")
        self.fx = lax.axis_index("fx")
        self.zh, self.core = self.fy // 2, self.fy % 2
        self.zl, self.y = self.fx // 4, self.fx % 4
        self.z = self.zh * 2 + self.zl

    def fx_at(self, a, b):
        return lax.rem(self.zl + a, 2) * 4 + lax.rem(self.y + b, 4)

    def fy_at(self, a, c):
        return lax.rem(self.zh + a, 2) * 2 + lax.rem(self.core + c, 2)

    def yz(self, a, b):
        z, y = lax.rem(self.z + a, 4), lax.rem(self.y + b, 4)
        dev = {"fy": (z // 2) * 2 + self.core, "fx": (z % 2) * 4 + y}
        return dev, y * 4 + z

    def dp_at(self, d):
        return lax.rem(self.dp + d, 4)


def rcopy(src, dst, ss, rs, dev):
    return pltpu.make_async_remote_copy(
        src_ref=src, dst_ref=dst, send_sem=ss, recv_sem=rs, device_id=dev, device_id_type=MESH
    )


def greet(devs):
    barrier = pltpu.get_barrier_semaphore()
    for dev in devs:
        pl.semaphore_signal(barrier, inc=1, device_id=dev, device_id_type=MESH)
    pl.semaphore_wait(barrier, len(devs))


def onehot(cond):
    return jnp.where(cond, 1.0, 0.0).astype(BF16)


def to_columns(rows, cols):
    n = rows * cols
    new = lax.broadcasted_iota(jnp.int32, (n, n), 0)
    old = lax.broadcasted_iota(jnp.int32, (n, n), 1)
    return onehot(old == lax.rem(new, rows) * cols + new // rows)


def attend(q, k, v, d, scale, mask):
    size, lanes = q.shape
    first = lax.broadcasted_iota(jnp.int32, (size, lanes), 1) < lanes // 2

    def stack(t):
        zero = jnp.zeros_like(t)
        return jnp.concatenate([jnp.where(first, t, zero), jnp.where(first, zero, t)], axis=0)

    def join(t):
        return jnp.where(first, t[:size], t[size:])

    qs = stack((q.astype(F32) * scale).astype(BF16))
    ds_ = stack(d)
    s = dims(qs, k, 1, 1)
    if mask is not None:
        s = jnp.where(mask, s, -1e30)
    e = jnp.exp(s - jnp.max(s, axis=-1, keepdims=True))
    w = e * (1.0 / jnp.sum(e, axis=-1, keepdims=True))
    wb = w.astype(BF16)
    out = join(dims(wb, v, 1, 0)).astype(BF16)
    dv = dims(wb, ds_, 0, 0).astype(BF16)
    gw = dims(ds_, v, 1, 1)
    inner = jnp.sum(w * gw, axis=-1, keepdims=True)
    gs = (w * (gw - inner)).astype(BF16)
    dq = (join(dims(gs, k, 1, 0)) * scale).astype(BF16)
    dk = dims(gs, qs, 0, 0).astype(BF16)
    return out, dq, dk, dv


class Reduce:
    @staticmethod
    def gathered(rows, nb):
        return (2, -(-(rows * nb // 16) // 16) * 256, LANES)

    @staticmethod
    def scratch(rows, nb):
        dma = pltpu.SemaphoreType.DMA
        piece = Reduce.gathered(rows, nb)[1] // 16
        return [
            pltpu.VMEM((4 * rows, nb * LANES), BF16),
            pltpu.VMEM((3, rows, nb * LANES), BF16),
            pltpu.VMEM((3, rows, nb * LANES), BF16),
            pltpu.VMEM((rows, nb * LANES), F32),
            pltpu.VMEM((16 * piece, LANES), BF16),
            pltpu.VMEM((3, 4 * piece, LANES), BF16),
            pltpu.VMEM((4 * piece, LANES), BF16),
            pltpu.VMEM((3, piece, LANES), BF16),
            dma((2,)), dma((5,)), dma((1,)), dma((1,)), dma((2,)), dma((2,)), dma((2,)), dma((2,)),
        ]

    def __init__(self, at, ag, refs, rows, nb, direct):
        self.ag = ag
        self.direct = direct
        (self.cx, self.xs, self.xr, self.acc, self.p16, self.ry, self.py, self.rz,
         self.c_s, self.c_r, self.x_s, self.x_r, self.r_s, self.r_r, self.g_s, self.g_r) = refs
        self.at, self.rows, self.nb = at, rows, nb
        self.piece = self.rz.shape[1]
        self.partner = {"fy": at.fy_at(0, 1)}

    def go(self, c):
        c.start()

    def x_block(self, d):
        return pl.ds(pl.multiple_of(self.at.dp_at(d) * self.rows, self.rows), self.rows)

    def swap_block(self, src, d):
        rows = self.x_block(d)
        return rcopy(src.at[rows], self.cx.at[rows], self.c_s.at[0], self.c_r.at[d], self.partner)

    def swap(self, src):
        for d in X_ORDER:
            self.swap_block(src, d).start()

    def along_x(self, mine, order=X_ORDER):
        for d in order:
            self.swap_block(self.cx, d).wait_recv()
            i = self.at.dp_at(d)
            block = self.x_block(d)
            value = mine(block) + self.cx[block, :].astype(F32)
            if d == 0:
                self.acc[...] = value
            else:
                self.xs[d - 1] = value.astype(BF16)
                rcopy(self.xs.at[d - 1], self.xr.at[d - 1], self.x_s.at[0], self.x_r.at[0], {"dp": i}).start()


    def ahead(self, z_first, k, stage):
        return self.at.yz(k, 0)[0] if z_first == (stage == 0) else self.at.yz(0, k)[0]

    def major(self, z_first):
        return self.at.z if z_first else self.at.y

    def minor(self, z_first):
        return self.at.y if z_first else self.at.z

    def column(self, z_first, k):
        size = 4 * self.piece
        return pl.ds(pl.multiple_of(lax.rem(self.major(z_first) + k, 4) * size, size), size)

    def slot(self, q):
        return pl.ds(pl.multiple_of(q * self.piece, self.piece), self.piece)

    def scatter(self, z_first):
        rcopy(self.xs, self.xr, self.x_s.at[0], self.x_r.at[0], self.partner).wait_recv()
        rows = self.rows
        for b in range(self.nb):
            lanes = slice(b * LANES, (b + 1) * LANES)
            value = self.acc[:, lanes]
            for d in range(3):
                value = value + self.xr[d, :, lanes].astype(F32)
            self.p16[b * rows : (b + 1) * rows, :] = value.astype(BF16)
        used = self.nb * rows
        if used < self.p16.shape[0]:
            self.p16[used:, :] = jnp.zeros((self.p16.shape[0] - used, LANES), BF16)
        for k in range(1, 4):
            src = self.p16.at[self.column(z_first, k)]
            rcopy(src, self.ry.at[k - 1], self.r_s.at[0], self.r_r.at[0], self.ahead(z_first, k, 0)).start()

    def scatter_again(self, z_first):
        rcopy(self.ry, self.ry, self.r_s.at[0], self.r_r.at[0], self.partner).wait_recv()
        value = self.p16[self.column(z_first, 0), :].astype(F32)
        for i in range(3):
            value = value + self.ry[i].astype(F32)
        self.py[...] = value.astype(BF16)
        for k in range(1, 4):
            src = self.py.at[self.slot(lax.rem(self.minor(z_first) + k, 4))]
            rcopy(src, self.rz.at[k - 1], self.r_s.at[1], self.r_r.at[1], self.ahead(z_first, k, 1)).start()

    def gather(self, z_first):
        at = self.at
        rcopy(self.rz, self.rz, self.r_s.at[1], self.r_r.at[1], self.partner).wait_recv()
        value = self.py[self.slot(self.minor(z_first)), :].astype(F32)
        for i in range(3):
            value = value + self.rz[i].astype(F32)
        mine = self.slot(self.major(z_first) * 4 + self.minor(z_first))
        self.ag[at.core, mine, :] = value.astype(BF16)
        src = self.ag.at[at.core, mine]
        if self.direct:
            for a, b in YZP:
                rcopy(src, src, self.g_s.at[1], self.g_r.at[1], at.yz(a, b)[0]).start()
            return
        for k in range(1, 4):
            rcopy(src, src, self.g_s.at[0], self.g_r.at[0], self.ahead(z_first, k, 1)).start()

    def pieces(self, stage):
        size = self.piece * (15 if self.direct else 12 if stage else 3)
        ref = self.ag.at[self.at.core, pl.ds(0, size)]
        return rcopy(ref, ref, self.g_s.at[stage], self.g_r.at[stage], self.partner)

    def gather_again(self, z_first):
        if self.direct:
            return
        self.pieces(0).wait_recv()
        src = self.ag.at[self.at.core, self.column(z_first, 0)]
        for k in range(1, 4):
            rcopy(src, src, self.g_s.at[1], self.g_r.at[1], self.ahead(z_first, k, 0)).start()

    def swap_back(self):
        self.pieces(1).wait_recv()
        ref = self.ag.at[self.at.core]
        rcopy(ref, ref, self.c_s.at[1], self.c_r.at[4], self.partner).start()

    def finish(self):
        ref = self.ag.at[1 - self.at.core]
        rcopy(ref, ref, self.c_s.at[1], self.c_r.at[4], self.partner).wait_recv()

    def drain(self):
        rcopy(self.cx, self.cx, self.c_s.at[0], self.c_r.at[0], self.partner).wait_send()
        rcopy(self.xs, self.xr, self.x_s.at[0], self.x_r.at[0], self.partner).wait_send()
        rcopy(self.ry, self.ry, self.r_s.at[0], self.r_r.at[0], self.partner).wait_send()
        rcopy(self.rz, self.rz, self.r_s.at[1], self.r_r.at[1], self.partner).wait_send()
        if not self.direct:
            self.pieces(0).wait_send()
        self.pieces(1).wait_send()
        ref = self.ag.at[self.at.core]
        rcopy(ref, ref, self.c_s.at[1], self.c_r.at[4], self.partner).wait_send()


class Legs:
    def __init__(self, at, rows, cols, sems):
        self.at, self.rows, self.cols = at, rows, cols
        self.row_s, self.row_r, self.col_s, self.col_r, self.loc = sems
        self.fx_dev = [{"fx": at.fx_at(a, b)} for a, b in FXP]
        self.fy_dev = [{"fy": at.fy_at(a, c)} for a, c in FYP]
        self.sent = []
        self.kept = []

    def gone(self, ref, ss, rs):
        self.sent.append(rcopy(ref, ref, ss, rs, self.fx_dev[0]))

    def keep(self, src, dst, sem):
        c = pltpu.make_async_copy(src, dst, sem)
        c.start()
        self.kept.append(c)

    def token_row(self, ref, u, owner):
        return ref.at[pl.ds(owner * 2 + u, 1)]

    def token_col(self, ref, u, owner):
        return ref.at[pl.ds(owner * (self.cols // 4) + u * (self.cols // 8), self.cols // 8)]

    def owner_row(self, ref, u, member):
        return ref.at[pl.ds(u, 1), pl.ds(member * self.cols, self.cols)]

    def owner_col(self, ref, u, member):
        return ref.at[pl.ds(u * (self.cols // 8), self.cols // 8), pl.ds(member * self.rows, self.rows)]

    def tokens_row(self, ref):
        return ref.at[pl.ds(0, 7)]

    def tokens_col(self, ref):
        return ref.at[pl.ds(0, 3 * (self.cols // 8))]

    def owners_row(self, ref, u):
        return ref.at[pl.ds(u, 1), pl.ds(0, 7 * self.cols)]

    def owners_col(self, ref, u):
        return ref.at[pl.ds(u * (self.cols // 8), self.cols // 8), pl.ds(0, 3 * self.rows)]

    def out_row(self, kind, u, src, dst):
        at, ss, rs = self.at, self.row_s.at[kind, u], self.row_r.at[kind, u]
        for i, (a, b) in enumerate(FXP):
            rcopy(
                self.token_row(src, u, at.fx_at(a, b)), self.owner_row(dst, u, at.fx), ss, rs, self.fx_dev[i]
            ).start()
        self.gone(self.tokens_row(src), ss, rs)
        self.keep(self.token_row(src, u, at.fx), self.owner_row(dst, u, at.fx), self.loc.at[kind, u])

    def out_col(self, kind, u, src, dst):
        at, ss, rs = self.at, self.col_s.at[kind, u], self.col_r.at[kind, u]
        for i, (a, c) in enumerate(FYP):
            rcopy(
                self.token_col(src, u, at.fy_at(a, c)), self.owner_col(dst, u, at.fy), ss, rs, self.fy_dev[i]
            ).start()
        self.gone(self.tokens_col(src), ss, rs)
        self.keep(self.token_col(src, u, at.fy), self.owner_col(dst, u, at.fy), self.loc.at[kind, 2 + u])

    def got_row(self, kind, u, dst):
        ref = self.owners_row(dst, u)
        rcopy(ref, ref, self.row_s.at[kind, u], self.row_r.at[kind, u], self.fx_dev[0]).wait_recv()

    def got_col(self, kind, u, dst):
        ref = self.owners_col(dst, u)
        rcopy(ref, ref, self.col_s.at[kind, u], self.col_r.at[kind, u], self.fx_dev[0]).wait_recv()

    def home_row(self, kind, u, src, dst):
        at, ss, rs = self.at, self.row_s.at[kind, u], self.row_r.at[kind, u]
        for i, (a, b) in enumerate(FXP):
            rcopy(
                self.owner_row(src, u, at.fx_at(a, b)), self.token_row(dst, u, at.fx), ss, rs, self.fx_dev[i]
            ).start()
        self.gone(self.owners_row(src, u), ss, rs)
        self.keep(self.owner_row(src, u, at.fx), self.token_row(dst, u, at.fx), self.loc.at[kind, u])

    def home_col(self, kind, u, src, dst):
        at, ss, rs = self.at, self.col_s.at[kind, u], self.col_r.at[kind, u]
        for i, (a, c) in enumerate(FYP):
            rcopy(
                self.owner_col(src, u, at.fy_at(a, c)), self.token_col(dst, u, at.fy), ss, rs, self.fy_dev[i]
            ).start()
        self.gone(self.owners_col(src, u), ss, rs)
        self.keep(self.owner_col(src, u, at.fy), self.token_col(dst, u, at.fy), self.loc.at[kind, 2 + u])

    def back_row(self, kind, u, dst):
        ref = self.tokens_row(dst)
        rcopy(ref, ref, self.row_s.at[kind, u], self.row_r.at[kind, u], self.fx_dev[0]).wait_recv()

    def back_col(self, kind, u, dst):
        ref = self.tokens_col(dst)
        rcopy(ref, ref, self.col_s.at[kind, u], self.col_r.at[kind, u], self.fx_dev[0]).wait_recv()

    def settle(self):
        for c in self.kept:
            c.wait()
        self.kept = []


def extra_devs(at):
    return [{"fy": at.fy_at(1, 0), "fx": at.fx_at(a, b)} for a, b in FXP]


N_RED = 16


def layer_kernel(
    rows, cols, scale, fine_h, cot_h, parent_h, coarse_h, level_h, table_h, gain_h, wq_h, wo_h,
    mixed_h, gfine_h, gcoarse_h, wsum_h, osum_h, small_h,
    parent, coarse, level, table, gain, fine, cot, wq, wo, tab, perm, pick, res, lv,
    sn, sd, snc, sdc, rown, rowd, coln, cold, qkv, grads, w2,
    orow, gnr, ocol, gnc, orow_t, gnr_t, ocol_t, gnc_t, dd, oo, gg,
    att, go_out, go_own, co_out, co_in, co_own, cf_out, cf_in, cz, cy_out, cy_in, cc_out, cc_in,
    sm_own, sm_in, sm_mid, sm_in2, mixed, gfine, gcoarse, wsum, osum, small,
    ld, st, ag_s, ag_r, fw_s, fw_r, row_s, row_r, col_s, col_r, loc,
    co_s, co_r, cf_s, cf_r, cy_s, cy_r, s1_s, s1_r, s2_s, s2_r, *red,
):
    at = Place()
    n, width = fine.shape
    half = width // 2
    own = coarse.shape[0]
    part = own // 2
    halfway = part * 8
    legs = Legs(at, rows, cols, (row_s, row_r, col_s, col_r, loc))
    fx_dev, fy_dev = legs.fx_dev, legs.fy_dev
    partner = fy_dev[0]
    dp_off = [(d, c) for d in range(4) for c in range(2) if (d, c) != (0, 0)]
    dp_dev = [{"dp": at.dp_at(d), "fy": at.fy_at(0, c)} for d, c in dp_off]
    weights = Reduce(at, wsum, red[:N_RED], width // 4, 3 * half // LANES, True)
    outs = Reduce(at, osum, red[N_RED:], width // 4, half // LANES, True)
    sent = legs.sent
    stores = []

    def store(src, dst):
        c = pltpu.make_async_copy(src, dst, st.at[len(stores)])
        c.start()
        stores.append(c)

    loads = [
        pltpu.make_async_copy(a, b, ld.at[i])
        for i, (a, b) in enumerate((
            (cot_h, cot), (wo_h, wo), (fine_h, fine), (wq_h, wq),
            (level_h, level), (table_h, table), (coarse_h, coarse), (parent_h, parent), (gain_h, gain),
        ))
    ]
    for i in (4, 5, 6, 7, 8, 0, 1, 2, 3):
        loads[i].start()
    for i in (4, 5, 6, 7, 8):
        loads[i].wait()
    as_row = onehot(lax.broadcasted_iota(jnp.int32, (8, own), 0) == level[...] + 1)
    same = lax.broadcasted_iota(jnp.int32, (8, LANES), 0) == lax.broadcasted_iota(jnp.int32, (8, LANES), 1)
    lev = dims(as_row, onehot(same), 0, 0)
    add = jnp.where(lev[:, 1:2] > 0.5, table[0:1, :], jnp.where(lev[:, 2:3] > 0.5, table[1:2, :], table[2:3, :]))
    summary = (coarse[...].astype(F32) + add).astype(BF16)
    for h in range(2):
        mine = pl.ds(h * halfway + at.fx * part, part)
        tab[mine, 0:width] = summary[h * part : (h + 1) * part]
        tab[mine, width : width + LANES] = lev[h * part : (h + 1) * part].astype(BF16)
    greet(fx_dev + fy_dev[1:] + extra_devs(at) + dp_dev)

    def chunk(owner, core):
        return tab.at[pl.ds(core * halfway + owner * part, part)]

    def across(a, b):
        fx = at.fx_at(a, b)
        return {"fx": fx} if a == 0 else {"fx": fx, "fy": at.fy_at(at.core, 0)}

    for i, (a, b) in enumerate(FXP):
        rcopy(chunk(at.fx, at.core), chunk(at.fx, at.core), ag_s.at[0], ag_r.at[i], across(a, b)).start()
    perm[...] = to_columns(rows, cols)
    p = parent[0]
    p = lax.rem(p, own) // part * halfway + p // own * part + lax.rem(p, part)
    token = lax.broadcasted_iota(jnp.int32, (n, rows), 0)
    spread = onehot(token // cols == lax.broadcasted_iota(jnp.int32, (n, rows), 1))
    high = dims(spread, (p // 16).astype(F32).astype(BF16), 1, 1)
    low = dims(spread, lax.rem(p, 16).astype(F32).astype(BF16), 1, 1)
    token = lax.broadcasted_iota(jnp.int32, high.shape, 0)
    reads = lax.rem(token, cols) // BLK == lax.broadcasted_iota(jnp.int32, high.shape, 1)
    ptok = jnp.sum(jnp.where(reads, high * 16.0 + low, 0.0), axis=-1, keepdims=True)
    pick[...] = onehot(lax.broadcasted_iota(jnp.int32, (n, n), 1).astype(F32) == ptok)
    loads[0].wait()
    loads[1].wait()
    d = dims(cot[...], wo[...], 1, 1).astype(BF16)
    sd[...] = d[:, 0:half].reshape(rows, cols, half)
    for u in range(2):
        legs.out_row(1, u, sd, rowd)
    sdc[...] = dims(perm[...], d[:, half:width], 1, 0).astype(BF16).reshape(cols, rows, half)
    for u in range(2):
        legs.out_col(1, u, sdc, cold)
    for i, (a, b) in enumerate(FXP):
        src = chunk(at.fx_at(a, 4 - b), at.core)
        rcopy(src, src, ag_s.at[0], ag_r.at[i], across(a, b)).wait_recv()
        rcopy(src, src, fw_s.at[0], fw_r.at[0], partner).start()
    loads[2].wait()
    seven = tab.at[pl.ds(0, 7 * part)]
    legs.gone(seven, ag_s.at[0], ag_r.at[0])
    legs.gone(seven, fw_s.at[0], fw_r.at[0])
    rcopy(seven, seven, fw_s.at[0], fw_r.at[0], partner).wait_recv()
    read = dims(pick[...], tab[...], 1, 0)
    lv[...] = read[:, width : width + LANES].astype(BF16)
    residual = fine[...].astype(F32) + read[:, 0:width]
    res[...] = residual
    inv = lax.rsqrt(jnp.mean(residual * residual, axis=-1, keepdims=True) + 1e-06)
    normed = (residual * inv * gain[...].reshape(1, width)).astype(BF16)
    sn[...] = normed.reshape(rows, cols, width)
    for u in range(2):
        legs.out_row(0, u, sn, rown)
    snc[...] = dims(perm[...], normed, 1, 0).astype(BF16).reshape(cols, rows, width)
    for u in range(2):
        legs.out_col(0, u, snc, coln)
    loads[3].wait()
    legs.settle()

    size = n // 2
    pair = 2 * 4 * rows
    i = lax.broadcasted_iota(jnp.int32, (2 * pair, pair), 0)
    j = lax.broadcasted_iota(jnp.int32, (2 * pair, pair), 1)
    mask = lax.rem(i, pair) // (4 * rows) == j // (4 * rows)

    def unit(which, u, x, d, out, gn, between=None):
        for j in range(3):
            c0 = (2 * j + which) * half
            qkv[:, j * half : (j + 1) * half] = dims(x, wq[:, c0 : c0 + half], 1, 0).astype(BF16)
        t_size = size if which == 0 else pair
        base = u * size

        def one(t, _):
            r = pl.ds(pl.multiple_of(t * t_size, t_size), t_size)
            for p in range(half // LANES):
                c = p * LANES
                q, k, v = (qkv[r, j * half + c : j * half + c + LANES] for j in range(3))
                o, dq, dk, dv = attend(q, k, v, d[r, c : c + LANES], scale, mask if which else None)
                out[r, c : c + LANES] = o
                g = pl.ds(pl.multiple_of(base + t * t_size, t_size), t_size)
                for j, value in enumerate((dq, dk, dv)):
                    grads[which, g, j * half + c : j * half + c + LANES] = value
            return 0

        if between is None:
            lax.fori_loop(0, size // t_size, one, 0)
        else:
            one(0, 0)
            between()
            lax.fori_loop(1, size // t_size, one, 0)
        total = None
        for j in range(3):
            c0 = (2 * j + which) * half
            g = grads[which, base : base + size, j * half : (j + 1) * half]
            back = dims(g, wq[:, c0 : c0 + half], 1, 1)
            total = back if total is None else total + back
        gn[...] = total.astype(BF16)

    def wgrad(which, x):
        for j in range(3):
            g = grads[which, :, j * half : (j + 1) * half]
            w2[which, :, j * half : (j + 1) * half] = dims(x, g, 0, 0).astype(BF16)

    for u in range(2):
        legs.got_row(1, u, rowd)
        legs.got_row(0, u, rown)
        unit(0, u, rown[u], rowd.at[u], orow.at[u], gnr.at[u])
    wgrad(0, rown[...].reshape(n, width))

    @pl.when(at.core == 1)
    def _():
        weights.swap(w2.at[0])

    for u in range(2):
        legs.got_col(1, u, cold)
        legs.got_col(0, u, coln)
        if u == 0:
            for v in range(2):
                legs.home_row(2, v, orow, orow_t)
            legs.home_row(3, 0, gnr, gnr_t)
        c4 = cols // 8
        x = coln[u * c4 : (u + 1) * c4].reshape(size, width)
        dd[...] = cold[u * c4 : (u + 1) * c4].reshape(size, half)
        def early():
            @pl.when(at.core == 0)
            def _():
                weights.along_x(lambda block: w2[0, block, :].astype(F32), X_ORDER[:2])

        unit(1, u, x, dd, oo, gg, early if u == 0 else None)
        ocol[u * c4 : (u + 1) * c4] = oo[...].reshape(c4, 4 * rows, half)
        gnc[u * c4 : (u + 1) * c4] = gg[...].reshape(c4, 4 * rows, width)
        legs.home_col(2, u, ocol, ocol_t)
        if u == 0:
            legs.home_row(3, 1, gnr, gnr_t)
        if u == 0:

            @pl.when(at.core == 0)
            def _():
                weights.along_x(lambda block: w2[0, block, :].astype(F32), X_ORDER[2:])

    wgrad(1, coln[...].reshape(n, width))
    legs.home_col(3, 0, gnc, gnc_t)


    @pl.when(at.core == 0)
    def _():
        weights.swap(w2.at[1])

    @pl.when(at.core == 0)
    def _():
        weights.scatter(False)

    @pl.when(at.core == 1)
    def _():
        weights.along_x(lambda block: w2[1, block, :].astype(F32))

    legs.home_col(3, 1, gnc, gnc_t)
    legs.settle()
    for u in range(2):
        legs.back_row(2, u, orow_t)
        legs.back_col(2, u, ocol_t)
    att[:, 0:half] = orow_t[...].reshape(n, half)
    att[:, half:width] = dims(perm[...], ocol_t[...].reshape(n, half), 0, 0).astype(BF16)

    def cot_half(h):
        return cot[:, pl.ds(pl.multiple_of(h * half, LANES), half)]

    go_out[...] = dims(att[...], cot_half(1 - at.core), 0, 0).astype(BF16)
    outs.swap(go_out)
    go_own[...] = dims(att[...], cot_half(at.core), 0, 0)
    mixed[...] = (res[...] + dims(att[...], wo[...], 1, 0)).astype(BF16)

    store(mixed, mixed_h)

    @pl.when(at.core == 0)
    def _():
        weights.scatter_again(False)

    outs.along_x(lambda block: go_own[block, :])

    @pl.when(at.core == 0)
    def _():
        weights.gather(False)

    for u in range(2):
        legs.back_row(3, u, gnr_t)
        legs.back_col(3, u, gnc_t)
    residual = res[...]
    grad_normed = gnr_t[...].reshape(n, width).astype(F32) + dims(perm[...], gnc_t[...].reshape(n, width), 0, 0)
    inv = lax.rsqrt(jnp.mean(residual * residual, axis=-1, keepdims=True) + 1e-06)
    pre = residual * inv
    sm_gain = jnp.sum(grad_normed * pre, axis=0, keepdims=True)
    g = grad_normed * gain[...].reshape(1, width)
    grad_residual = inv * (g - pre * jnp.mean(g * pre, axis=-1, keepdims=True)) + cot[...].astype(F32)
    gf = grad_residual.astype(BF16)
    gfine[...] = gf

    def dense(core):
        return dims(pick[:, pl.ds(pl.multiple_of(core * halfway, LANES), halfway)], gfine[...], 0, 0)

    co_out[...] = dense(1 - at.core).astype(BF16)
    rcopy(co_out, co_in, co_s.at[0], co_r.at[0], partner).start()
    legs.gone(co_out, co_s.at[0], co_r.at[0])
    levels = dims(lv[...], gfine[...], 0, 0)[0:8]
    row = lax.broadcasted_iota(jnp.int32, (8, half), 0)
    for h in range(2):
        c = h * half
        both = jnp.where(row == 0, sm_gain[:, c : c + half], levels[:, c : c + half])
        sm_own[4 * h : 4 * h + 4, :] = both[0:4]
    for i, dev in enumerate(dp_dev):
        rcopy(sm_own, sm_in.at[i], s1_s.at[0], s1_r.at[0], dev).start()
    co_own[...] = dense(at.core)
    store(gfine, gfine_h)

    @pl.when(at.core == 0)
    def _():
        weights.gather_again(False)

    rcopy(co_out, co_in, co_s.at[0], co_r.at[0], partner).wait_recv()

    def block(zl, y):
        return pl.ds(pl.multiple_of((zl * 4 + y) * part, part), part)

    for b in range(1, 4):
        dev, _ = at.yz(0, b)
        y = lax.rem(at.y + b, 4)
        for zl in range(2):
            rows_ = block(zl, y)
            cf_out[b - 1, zl] = (co_own[rows_, :] + co_in[rows_, :].astype(F32)).astype(BF16)
        rcopy(cf_out.at[b - 1], cf_in.at[b - 1], cf_s.at[0], cf_r.at[0], dev).start()

    @pl.when(at.core == 1)
    def _():
        weights.scatter(True)

    outs.scatter(True)
    rcopy(sm_in, sm_in, s1_s.at[0], s1_r.at[0], partner).wait_recv()
    total = sm_own[...]
    for i in range(7):
        total = total + sm_in[i]
    sm_mid[0] = total
    for i in range(3):
        dev, _ = at.yz(i + 1, 0)
        rcopy(sm_mid.at[0], sm_in2.at[0, i], s2_s.at[0], s2_r.at[0], dev).start()

    @pl.when(at.core == 1)
    def _():
        weights.scatter_again(True)

    outs.scatter_again(True)
    rcopy(cf_in, cf_in, cf_s.at[0], cf_r.at[0], partner).wait_recv()
    for zl in range(2):
        rows_ = block(zl, at.y)
        value = co_own[rows_, :] + co_in[rows_, :].astype(F32)
        for i in range(3):
            value = value + cf_in[i, zl].astype(F32)
        cz[zl] = value
        cy_out[zl] = value.astype(BF16)
    for a in range(1, 4):
        dev, _ = at.yz(a, 0)
        rcopy(cy_out.at[lax.rem(at.zl + a, 2)], cy_in.at[a - 1], cy_s.at[0], cy_r.at[0], dev).start()

    @pl.when(at.core == 0)
    def _():
        weights.swap_back()

    rcopy(sm_in2.at[0], sm_in2.at[0], s2_s.at[0], s2_r.at[0], partner).wait_recv()
    sm_mid[1] = sm_mid[0] + sm_in2[0, 0] + sm_in2[0, 1] + sm_in2[0, 2]
    for i in range(3):
        dev, _ = at.yz(0, i + 1)
        rcopy(sm_mid.at[1], sm_in2.at[1, i], s2_s.at[1], s2_r.at[1], dev).start()

    @pl.when(at.core == 1)
    def _():
        weights.gather(True)

    outs.gather(True)
    rcopy(cy_in, cy_in, cy_s.at[0], cy_r.at[0], partner).wait_recv()
    value = cz[at.zl] + cy_in[0].astype(F32) + cy_in[1].astype(F32) + cy_in[2].astype(F32)
    gcoarse[pl.ds(pl.multiple_of(at.core * part, part), part), :] = value
    cc_out[...] = value.astype(BF16)
    rcopy(cc_out, cc_in, co_s.at[1], co_r.at[1], partner).start()

    @pl.when(at.core == 1)
    def _():
        weights.gather_again(True)

    outs.gather_again(True)
    rcopy(cc_out, cc_in, co_s.at[1], co_r.at[1], partner).wait_recv()
    gcoarse[pl.ds(pl.multiple_of((1 - at.core) * part, part), part), :] = cc_in[...].astype(F32)
    store(gcoarse, gcoarse_h)
    rcopy(sm_in2.at[1], sm_in2.at[1], s2_s.at[1], s2_r.at[1], partner).wait_recv()
    small[...] = sm_mid[1] + sm_in2[1, 0] + sm_in2[1, 1] + sm_in2[1, 2]
    store(small, small_h)

    @pl.when(at.core == 1)
    def _():
        weights.swap_back()

    outs.swap_back()
    weights.finish()
    store(wsum, wsum_h)
    outs.finish()
    store(osum, osum_h)
    legs.gone(sm_in, s1_s.at[0], s1_r.at[0])
    legs.gone(cf_in, cf_s.at[0], cf_r.at[0])
    legs.gone(cy_in, cy_s.at[0], cy_r.at[0])
    legs.gone(cc_in, co_s.at[1], co_r.at[1])
    legs.gone(sm_in2.at[0], s2_s.at[0], s2_r.at[0])
    legs.gone(sm_in2.at[1], s2_s.at[1], s2_r.at[1])
    legs.settle()
    for c in sent:
        c.wait_send()
    weights.drain()
    outs.drain()
    for c in stores:
        c.wait()


def layer(fine, cot, parent, coarse, level, table, gain, wq, wo, rows, cols, scale):
    n, width = fine.shape
    half = width // 2
    own = coarse.shape[0]
    part = own // 2
    dma = pltpu.SemaphoreType.DMA
    vmem = pltpu.VMEM
    hbm = pl.BlockSpec(memory_space=pl.ANY)
    r2, c8, c4 = rows // 8, cols * 8, cols // 4
    return pl.pallas_call(
        functools.partial(layer_kernel, rows, cols, scale),
        name="layer",
        out_shape=[
            jax.ShapeDtypeStruct((n, width), BF16),
            jax.ShapeDtypeStruct((n, width), BF16),
            jax.ShapeDtypeStruct((own, width), F32),
            jax.ShapeDtypeStruct(Reduce.gathered(width // 4, 3 * half // LANES), BF16),
            jax.ShapeDtypeStruct(Reduce.gathered(width // 4, half // LANES), BF16),
            jax.ShapeDtypeStruct((8, half), F32),
        ],
        in_specs=[hbm] * 2 + [pl.BlockSpec(memory_space=pltpu.MemorySpace.HBM)] * 5 + [hbm] * 2,
        out_specs=[hbm] * 6,
        scratch_shapes=[
            vmem(parent.shape, jnp.int32), vmem((own, width), BF16), vmem(level.shape, jnp.int32),
            vmem(table.shape, F32), vmem(gain.shape, F32),
            vmem((n, width), BF16), vmem((n, width), BF16), vmem((width, 6 * half), BF16), vmem((width, width), BF16),
            vmem((8 * own, width + LANES), BF16), vmem((n, n), BF16), vmem((n, n), BF16), vmem((n, width), F32), vmem((n, LANES), BF16),
            vmem((rows, cols, width), BF16), vmem((rows, cols, half), BF16),
            vmem((cols, rows, width), BF16), vmem((cols, rows, half), BF16),
            vmem((r2, c8, width), BF16), vmem((r2, c8, half), BF16),
            vmem((c4, rows * 4, width), BF16), vmem((c4, rows * 4, half), BF16),
            vmem((n // 2, 3 * half), BF16), vmem((2, n, 3 * half), BF16), vmem((2, width, 3 * half), BF16),
            vmem((r2, c8, half), BF16), vmem((r2, c8, width), BF16),
            vmem((c4, rows * 4, half), BF16), vmem((c4, rows * 4, width), BF16),
            vmem((rows, cols, half), BF16), vmem((rows, cols, width), BF16),
            vmem((cols, rows, half), BF16), vmem((cols, rows, width), BF16),
            vmem((n // 2, half), BF16), vmem((n // 2, half), BF16), vmem((n // 2, width), BF16),
            vmem((n, width), BF16), vmem((width, half), BF16), vmem((width, half), F32),
            vmem((8 * part, width), BF16), vmem((8 * part, width), BF16), vmem((8 * part, width), F32),
            vmem((3, 2, part, width), BF16), vmem((3, 2, part, width), BF16), vmem((2, part, width), F32),
            vmem((2, part, width), BF16), vmem((3, part, width), BF16),
            vmem((part, width), BF16), vmem((part, width), BF16),
            vmem((8, half), F32), vmem((7, 8, half), F32), vmem((2, 8, half), F32), vmem((2, 3, 8, half), F32),
            vmem((n, width), BF16), vmem((n, width), BF16), vmem((own, width), F32),
            vmem(Reduce.gathered(width // 4, 3 * half // LANES), BF16),
            vmem(Reduce.gathered(width // 4, half // LANES), BF16), vmem((8, half), F32),
            dma((9,)), dma((6,)), dma((1,)), dma((7,)), dma((1,)), dma((1,)),
            dma((4, 2)), dma((4, 2)), dma((4, 2)), dma((4, 2)), dma((4, 4)),
            dma((2,)), dma((2,)), dma((1,)), dma((1,)), dma((1,)), dma((1,)),
            dma((1,)), dma((1,)), dma((2,)), dma((2,)),
            *Reduce.scratch(width // 4, 3 * half // LANES),
            *Reduce.scratch(width // 4, half // LANES),
        ],
        compiler_params=pltpu.CompilerParams(
            collective_id=0, has_side_effects=True, vmem_limit_bytes=VMEM_LIMIT
        ),
    )(fine, cot, parent, coarse, level, table, gain, wq, wo)


def emit_kernel(
    rows, grad_scale, mixed_h, gfine_h, gcoarse_h, wsum_h, osum_h, small_h,
    mixed_o, gfine_o, gcoarse_o, gq_o, gout_o, ggain, glevel,
    mixed, gfine, gcoarse, wsum, osum, small, gq, gout, ld, st,
):
    ins = ((wsum_h, wsum), (osum_h, osum), (small_h, small), (mixed_h, mixed), (gfine_h, gfine), (gcoarse_h, gcoarse))
    loads = [pltpu.make_async_copy(a, b, ld.at[i]) for i, (a, b) in enumerate(ins)]
    outs = ((gq, gq_o), (gout, gout_o), (mixed, mixed_o), (gfine, gfine_o), (gcoarse, gcoarse_o))
    stores = [pltpu.make_async_copy(a, b, st.at[i]) for i, (a, b) in enumerate(outs)]
    for c in loads:
        c.start()
    half = small.shape[1]
    nb = half // LANES
    loads[0].wait()
    for h in range(2):
        for j in range(3):
            for b in range(nb):
                c = (2 * j + h) * half + b * LANES
                k = (j * nb + b) * rows
                gq[:, c : c + LANES] = wsum[h, k : k + rows, :].astype(F32) * grad_scale
    stores[0].start()
    for i in range(3):
        loads[3 + i].wait()
        stores[2 + i].start()
    loads[1].wait()
    for h in range(2):
        for b in range(nb):
            c = h * half + b * LANES
            gout[:, c : c + LANES] = osum[h, b * rows : (b + 1) * rows, :].astype(F32) * grad_scale
    stores[1].start()
    loads[2].wait()
    for h in range(2):
        glevel[:, h * half : (h + 1) * half] = small[4 * h + 1 : 4 * h + 4, :] * grad_scale
    dp = lax.axis_index("dp")
    vector = jnp.concatenate([small[0:1, :], small[4:5, :]], axis=1) * grad_scale
    share = vector[:, 0:rows]
    for i in range(1, 4):
        share = jnp.where(dp == i, vector[:, i * rows : (i + 1) * rows], share)
    ggain[...] = share
    for c in stores:
        c.wait()


def emit(parts, grad_scale):
    mixed, gfine, gcoarse, wsum, osum, small = parts
    n, width = mixed.shape
    rows = width // 4
    here = pl.BlockSpec(memory_space=pltpu.VMEM)
    far = pl.BlockSpec(memory_space=pl.ANY)
    shapes = [
        jax.ShapeDtypeStruct(mixed.shape, BF16),
        jax.ShapeDtypeStruct(gfine.shape, BF16),
        jax.ShapeDtypeStruct(gcoarse.shape, F32),
        jax.ShapeDtypeStruct((rows, 3 * width), F32),
        jax.ShapeDtypeStruct((rows, width), F32),
        jax.ShapeDtypeStruct((1, rows), F32),
        jax.ShapeDtypeStruct((LEVELS, width), F32),
    ]
    return pl.pallas_call(
        functools.partial(emit_kernel, rows, grad_scale),
        name="emit",
        out_shape=shapes,
        in_specs=[far] * 6,
        out_specs=[far] * 5 + [here] * 2,
        scratch_shapes=[
            *[pltpu.VMEM(p.shape, p.dtype) for p in parts],
            pltpu.VMEM(shapes[3].shape, F32), pltpu.VMEM(shapes[4].shape, F32),
            pltpu.SemaphoreType.DMA((6,)), pltpu.SemaphoreType.DMA((5,)),
        ],
        compiler_params=pltpu.CompilerParams(vmem_limit_bytes=EMIT_LIMIT),
    )(*parts)


def local(
    fine_tokens,
    parent,
    coarse_tokens,
    tile_level,
    level_table,
    norm_gain,
    qkv_weight,
    out_weight,
    cotangent,
):
    _, rows, cols, width = fine_tokens.shape
    half = width // 2
    n = rows * cols
    own = coarse_tokens.shape[1]
    scale = (width // HEADS) ** (-0.5)
    total_tokens = n * lax.axis_size("dp") * lax.axis_size("fy") * lax.axis_size("fx")
    grad_scale = 1.0 / math.sqrt(total_tokens)
    fine = fine_tokens.reshape(n, width)
    cot = cotangent.reshape(n, width)
    parts = layer(
        fine, cot, parent.swapaxes(1, 2), coarse_tokens.reshape(own, width), tile_level,
        level_table, norm_gain, qkv_weight, out_weight, rows, cols, scale,
    )
    mixed, gfine, gcoarse, gq, gout, ggain, glevel = emit(parts, grad_scale)
    return (
        mixed.reshape(fine_tokens.shape),
        gfine.reshape(fine_tokens.shape),
        gcoarse[None],
        gq,
        gout,
        ggain.reshape(-1),
        glevel,
    )


def solution(mesh):
    return jax.shard_map(
        local,
        mesh=mesh,
        in_specs=(
            P("dp", "fy", "fx", None),
            P("dp", "fy", "fx"),
            P("dp", "fx", None),
            P("dp", "fx"),
            P(),
            P(),
            P(),
            P(),
            P("dp", "fy", "fx", None),
        ),
        out_specs=(
            P("dp", "fy", "fx", None),
            P("dp", "fy", "fx", None),
            P("dp", "fx", None),
            P("dp", None),
            P("dp", None),
            P("dp"),
            P(),
        ),
        check_vma=False,
    )
```
